32 devices in a mesh: depth: 8 (over z, y), rows: 4 (over x, core).
Axes of the slice: x: 2, y: 2, z: 4, core: 2. Of those that a mesh axis runs over, the one named last changes fastest.
Arguments:
- density: float32 [4, 256, 8192], P('rows', 'depth'), may hold values from 0.00078125 to 0.015625
- attenuation: float32 [4, 256, 8192], P('rows', 'depth'), may hold values from 0.00078125 to 0.015625
- measured: float32 [4, 4, 8192], P(None, 'rows'), may hold values from -3 to 3
- angle_ids: int32 [4], replicated, may hold values from 0 to 359
- sides: int32 [4], replicated, may hold values from 0 to 1, as said below
Outputs:
- grad_density: float32 [4, 256, 8192], P('rows', 'depth')
- grad_attenuation: float32 [4, 256, 8192], P('rows', 'depth')
The draws below stay inside these ranges and needn't reach their ends.
Inputs may be any that keep to these rules, and one draw needn't show every extreme that they name: Half of the 4 views have sides 1.
All inputs are finite; a program needn't handle non-finite values.
Results may differ from the reference program's by a relative error of at most 0.0001.
Values sent between devices are 32-bit elements; how exact they have to be, the bound alone decides.
No kernel may reach another device: no remote copies, remote signals or barrier semaphores. Data moves between devices by JAX's collectives and lax.ppermute only.
A program may use at most 64 MiB of HBM per device.

```python
import math
import jax
import jax.numpy as jnp
from jax import lax

C = 8192
VIEWS = 4
ANGLES = 360
NZ = 256
NR = 4


def draw_sides(key, part):
    return jax.random.permutation(key, jnp.arange(VIEWS) % 2).astype(jnp.int32)


def touch_ends(entries, key, smallest, top_value):
    extent = entries.shape
    place = [jax.random.randint(jax.random.fold_in(key, axis), (), 0, extent[axis]) for axis in range(len(extent))]
    entries = entries.at[tuple(place)].set(smallest)
    longest = extent.index(max(extent))
    place[longest] = (place[longest] + 1) % extent[longest]
    return entries.at[tuple(place)].set(top_value)


def shard_levels(rng, dims, pieces, smallest, top_value):
    def one(axis_at, shards_of):
        steps = jax.random.uniform(jax.random.fold_in(jax.random.fold_in(rng, 6), axis_at), (shards_of,), jnp.float32, smallest / len(pieces), top_value / len(pieces))
        return jnp.repeat(jnp.exp(steps), dims[axis_at] // shards_of).reshape((-1,) + (1,) * (len(dims) - axis_at - 1))

    gain = one(*pieces[0])
    for cut in pieces[1:]:
        gain = gain * one(*cut)
    return gain


def gaussian(rng, shape, scale, reach, pieces=(), held_as=jnp.bfloat16):
    drawn = jax.random.normal(rng, shape, jnp.float32) * scale
    if len(pieces) > 0:
        drawn = shard_levels(rng, shape, pieces, -0.22, 0.18) * drawn
    return jnp.clip(drawn, min=-reach, max=reach).astype(held_as)


def setup_inputs(seed: int = 0) -> dict:
    arg_keys = jax.random.split(jax.random.key(seed), 6)
    return {
        "density": jnp.clip(jnp.exp(math.log(0.015625) - 2.9957323 * jax.random.uniform(arg_keys[0], (NR, NZ, C), jnp.float32) ** shard_levels(arg_keys[0], (NR, NZ, C), ((0, 4), (1, 8)), -0.2, 0.2)), 0.00078125, 0.015625),
        "attenuation": jnp.clip(jnp.exp(math.log(0.015625) - 2.9957323 * jax.random.uniform(arg_keys[1], (NR, NZ, C), jnp.float32) ** shard_levels(arg_keys[1], (NR, NZ, C), ((0, 4), (1, 8)), -0.2, 0.2)), 0.00078125, 0.015625),
        "measured": gaussian(arg_keys[2], (VIEWS, NR, C), 0.5, 3.0, ((1, 4),), jnp.float32),
        "angle_ids": touch_ends(jax.random.randint(arg_keys[3], (VIEWS,), 0, ANGLES), jax.random.fold_in(arg_keys[3], 1), 0, ANGLES - 1).astype(jnp.int32),
        "sides": draw_sides(jax.random.fold_in(arg_keys[5], 71), 0),
    }


def tilt_angle(angle_ids):
    return 0.8 * jnp.sin(jnp.pi * (angle_ids.astype(jnp.float32) + 0.5) / ANGLES - jnp.pi / 2)


def shifted_pair(field):
    widths = [(0, 0)] * (field.ndim - 1)
    from_left = jnp.pad(field[..., :-1], widths + [(1, 0)])
    from_right = jnp.pad(field[..., 1:], widths + [(0, 1)])
    return from_left, from_right


def resample(field, tilting):
    from_left, from_right = shifted_pair(field)
    return (1.0 - jnp.abs(tilting)) * field + jnp.maximum(tilting, 0.0) * from_left + jnp.maximum(-tilting, 0.0) * from_right


def resample_back(field, tilting):
    from_left, from_right = shifted_pair(field)
    return (1.0 - jnp.abs(tilting)) * field + jnp.maximum(tilting, 0.0) * from_right + jnp.maximum(-tilting, 0.0) * from_left


def forward_row(density_row, attenuation_row, tilting, far_side):
    emission = resample(density_row, tilting)
    absorb = resample(attenuation_row, tilting)
    running = jnp.cumsum(absorb, axis=0)
    depth_sum = jnp.where(far_side, running[-1:] - running, running - absorb)
    transmit = jnp.exp(-depth_sum)
    radiance = emission * transmit
    return transmit, radiance


def detector_blur(image):
    padded = jnp.pad(image, ((0, 0), (1, 1), (0, 0)))
    return 0.25 * padded[:, :-2] + 0.5 * padded[:, 1:-1] + 0.25 * padded[:, 2:]


def reference(density, attenuation, measured, angle_ids, sides):
    tilts = tilt_angle(angle_ids)
    far_flags = sides == 1

    def first_pass(row_pair):
        density_row, attenuation_row = row_pair
        signals = []
        for view in range(VIEWS):
            transmit, radiance = forward_row(density_row, attenuation_row, tilts[view], far_flags[view])
            signals.append(jnp.sum(radiance, axis=0))
        return jnp.stack(signals)

    signal = jnp.transpose(lax.map(first_pass, (density, attenuation)), (1, 0, 2))
    residual = detector_blur(signal) - measured
    back_signal = jnp.transpose(detector_blur(residual), (1, 0, 2))
    signal_rows = jnp.transpose(signal, (1, 0, 2))

    def second_pass(row_items):
        density_row, attenuation_row, back_row, signal_row = row_items
        grad_emit = jnp.zeros(density_row.shape, jnp.float32)
        grad_absorb = jnp.zeros(density_row.shape, jnp.float32)
        for view in range(VIEWS):
            transmit, radiance = forward_row(density_row, attenuation_row, tilts[view], far_flags[view])
            emitted_before = jnp.cumsum(radiance, axis=0) - radiance
            behind = jnp.where(far_flags[view], emitted_before, signal_row[view][None] - emitted_before - radiance)
            grad_emit = grad_emit + resample_back(back_row[view][None] * transmit, tilts[view])
            grad_absorb = grad_absorb + resample_back(-back_row[view][None] * behind, tilts[view])
        return grad_emit, grad_absorb

    grad_density, grad_attenuation = lax.map(second_pass, (density, attenuation, back_signal, signal_rows))
    return grad_density, grad_attenuation
```

```python
import functools
import math

import jax
import jax.numpy as jnp
from jax import lax
from jax.experimental import pallas as pl
from jax.experimental.pallas import tpu as pltpu
from jax.sharding import PartitionSpec as P

ANGLES = 360
PAD = 128
F32 = jnp.float32
BF16 = jnp.bfloat16


def tilt_parts(angle):
    tilt = 0.8 * jnp.sin(jnp.pi * (angle.astype(F32) + 0.5) / ANGLES - jnp.pi / 2)
    return 1.0 - jnp.abs(tilt), jnp.maximum(tilt, 0.0), jnp.maximum(-tilt, 0.0)


def view_column(ref, views, shape):
    rows = lax.broadcasted_iota(jnp.int32, shape, 0)
    out = jnp.full(shape, ref[0], jnp.int32)
    for v in range(1, views):
        out = jnp.where(rows == v, ref[v], out)
    return out


def strict_sums(rows, cells, first):
    i = lax.broadcasted_iota(jnp.int32, (rows, 2 * cells), 0)
    j = lax.broadcasted_iota(jnp.int32, (rows, 2 * cells), 1)
    j = jnp.where(j >= cells, j - cells, j)
    below = jnp.where(first, (j < i).astype(jnp.int32), (j > i).astype(jnp.int32))
    return jnp.where(i >= cells, 1, below).astype(F32).astype(BF16)


def two_terms(value):
    high = value.astype(BF16)
    low = (value - high.astype(F32)).astype(BF16)
    return jnp.concatenate([high, low], axis=0)


def neighbours(block):
    width = block.shape[-1]
    inner = slice(PAD, width - PAD)
    return pltpu.roll(block, 1, 1)[:, inner], pltpu.roll(block, width - 1, 1)[:, inner]


def slab_kernel(views, wide, angle_ref, side_ref, place_ref, d_ref, a_ref, m_ref, up_ref, lt_ref, lb_ref, x_ref, t_ref, e_ref):
    cells, columns = d_ref.shape
    chunks = columns // wide
    lower = strict_sums(cells + 8, cells, True)
    upper = strict_sums(cells + 8, cells, False)
    for ref in (x_ref, e_ref):
        for edge in (0, PAD + columns):
            ref[..., pl.ds(edge, PAD)] = jnp.zeros(ref.shape[:-1] + (PAD,), F32)
    for edge in (0, PAD + columns):
        t_ref[:, pl.ds(edge, PAD)] = jnp.zeros((8, PAD), F32)

    def sums(j, carry):
        at = pl.multiple_of(j * wide, PAD)
        into = pl.ds(pl.multiple_of(at + PAD, PAD), wide)
        terms = two_terms(a_ref[:, pl.ds(at, wide)])
        below = jnp.dot(lower, terms, preferred_element_type=F32)
        above = jnp.dot(upper, terms, preferred_element_type=F32)
        x_ref[0, 0, :, into] = below[:cells]
        x_ref[0, 1, :, into] = above[:cells]
        t_ref[:, into] = below[cells:]
        e_ref[0, :, into] = d_ref[:, pl.ds(at, wide)]
        return carry

    lax.fori_loop(0, chunks, sums, 0)

    def shifts(j, carry):
        at = pl.multiple_of(j * wide, PAD)
        around = pl.ds(at, wide + 2 * PAD)
        into = pl.ds(pl.multiple_of(at + PAD, PAD), wide)
        for side in range(2):
            left, right = neighbours(x_ref[0, side, :, around])
            x_ref[1, side, :, into] = left
            x_ref[2, side, :, into] = right
        left, right = neighbours(e_ref[0, :, around])
        e_ref[1, :, into] = left
        e_ref[2, :, into] = right
        return carry

    lax.fori_loop(0, chunks, shifts, 0)

    centres, besides, behind_sums = [], [], []
    for v in range(views):
        centre, left, right = tilt_parts(jnp.full((8, 128), angle_ref[v], jnp.int32))
        centres.append(centre[:1, :1])
        besides.append((left + right)[:1, :1])
        behind_sums.append(jnp.where(side_ref[v] == 1, lower.astype(F32), upper.astype(F32)).astype(BF16))
    place = lax.rem(place_ref[0], views)

    def rays(j, carry):
        at = pl.multiple_of(j * wide, PAD)
        into = pl.ds(pl.multiple_of(at + PAD, PAD), wide)
        rows = []
        for v in range(views):
            shift = jnp.where(angle_ref[v] * 2 >= ANGLES, 1, 2)
            depth = centres[v] * x_ref[0, side_ref[v], :, into] + besides[v] * x_ref[shift, side_ref[v], :, into]
            light = jnp.exp(-depth)
            emission = centres[v] * e_ref[0, :, into] + besides[v] * e_ref[shift, :, into]
            behind = jnp.dot(behind_sums[v], two_terms(emission * light), preferred_element_type=F32)
            lt_ref[v, :, pl.ds(at, wide)] = light
            lb_ref[v, :, pl.ds(at, wide)] = behind[:cells]
            rows.append(behind[cells : cells + 1])
        left, right = neighbours(t_ref[:, pl.ds(at, wide + 2 * PAD)])
        rows += [left[:1], t_ref[:1, into], right[:1], m_ref[pl.ds(place, 1), pl.ds(at, wide)]]
        up_ref[j] = jnp.concatenate(rows, axis=0)
        return carry

    lax.fori_loop(0, chunks, rays, 0)


def column_kernel(views, slabs, rows, angle_ref, side_ref, up_ref, down_ref):
    wide = up_ref.shape[-1]
    shape = (views, wide)
    centre, left, right = tilt_parts(view_column(angle_ref, views, shape))
    far = view_column(side_ref, views, shape) == 1
    passes, behinds, signals = {}, {}, []
    for r in range(rows):
        absorbs, runs = [], []
        run = jnp.zeros(shape, F32)
        for k in range(slabs):
            block = up_ref[k * rows + r]
            absorb = left * block[views : views + 1] + centre * block[views + 1 : views + 2] + right * block[views + 2 : views + 3]
            runs.append(run)
            absorbs.append(absorb)
            run = run + absorb
        radiances, starts = [], []
        signal = jnp.zeros(shape, F32)
        for k in range(slabs):
            entering = jnp.where(far, run - runs[k] - absorbs[k], runs[k])
            passes[k, r] = jnp.exp(-entering)
            radiance = passes[k, r] * up_ref[k * rows + r][:views]
            starts.append(signal)
            radiances.append(radiance)
            signal = signal + radiance
        for k in range(slabs):
            behinds[k, r] = jnp.where(far, starts[k], signal - starts[k] - radiances[k])
        signals.append(signal)

    def blur(values):
        out = []
        for r in range(rows):
            total = 0.5 * values[r]
            if r > 0:
                total = total + 0.25 * values[r - 1]
            if r + 1 < rows:
                total = total + 0.25 * values[r + 1]
            out.append(total)
        return out

    residuals = []
    for r, value in enumerate(blur(signals)):
        seen = jnp.concatenate([up_ref[v * rows + r][views + 3 : views + 4] for v in range(views)], axis=0)
        residuals.append(value - seen)
    for r, back in enumerate(blur(residuals)):
        for k in range(slabs):
            scaled = back * behinds[k, r]
            parts = [back * passes[k, r]]
            for weight in (centre, left, right):
                parts.append(jnp.sum(weight * scaled, axis=0, keepdims=True))
            parts.append(jnp.zeros((1, wide), F32))
            down_ref[k * rows + r] = jnp.concatenate(parts, axis=0)


def gradient_kernel(views, wide, angle_ref, down_ref, lt_ref, lb_ref, gd_ref, ga_ref, p_ref):
    cells, columns = gd_ref.shape
    chunks = columns // wide
    for edge in (0, PAD + columns):
        p_ref[..., pl.ds(edge, PAD)] = jnp.zeros(p_ref.shape[:-1] + (PAD,), F32)
    weights = []
    for v in range(views):
        weights.append([part[:1, :1] for part in tilt_parts(jnp.full((8, 128), angle_ref[v], jnp.int32))])

    def products(j, carry):
        at = pl.multiple_of(j * wide, PAD)
        into = pl.ds(pl.multiple_of(at + PAD, PAD), wide)
        block = down_ref[j]
        density = [None] * 3
        absorb = [jnp.broadcast_to(block[views + i : views + i + 1], (cells, wide)) for i in range(3)]
        for v in range(views):
            light = lt_ref[v, :, pl.ds(at, wide)]
            behind = lb_ref[v, :, pl.ds(at, wide)]
            for i in range(3):
                scale = weights[v][i] * block[v : v + 1]
                density[i] = scale * light if density[i] is None else density[i] + scale * light
                absorb[i] = absorb[i] + scale * behind
        for i in range(3):
            p_ref[0, i, :, into] = density[i]
            p_ref[1, i, :, into] = absorb[i]
        return carry

    lax.fori_loop(0, chunks, products, 0)

    def shifts(j, carry):
        at = pl.multiple_of(j * wide, PAD)
        around = pl.ds(at, wide + 2 * PAD)
        into = pl.ds(pl.multiple_of(at + PAD, PAD), wide)
        for q, (ref, sign) in enumerate(((gd_ref, 1.0), (ga_ref, -1.0))):
            after = neighbours(p_ref[q, 1, :, around])[1]
            before = neighbours(p_ref[q, 2, :, around])[0]
            ref[:, pl.ds(at, wide)] = sign * (p_ref[q, 0, :, into] + after + before)
        return carry

    lax.fori_loop(0, chunks, shifts, 0)


def on_device(density, attenuation, measured, angle_ids, sides):
    cells, columns = density.shape[1:]
    views = measured.shape[0]
    slabs, rows = lax.axis_size("depth"), lax.axis_size("rows")
    devices = slabs * rows
    part = columns // devices
    wide = part if part % PAD == 0 else 2 * PAD
    smem = pl.BlockSpec(memory_space=pltpu.SMEM)
    vmem = pl.BlockSpec(memory_space=pltpu.VMEM)
    place = lax.axis_index("depth").astype(jnp.int32)[None]
    padded = columns + 2 * PAD
    up, light, behind = pl.pallas_call(
        functools.partial(slab_kernel, views, wide),
        out_shape=(
            jax.ShapeDtypeStruct((columns // wide, views + 4, wide), F32),
            jax.ShapeDtypeStruct((views, cells, columns), F32),
            jax.ShapeDtypeStruct((views, cells, columns), F32),
        ),
        in_specs=[smem] * 3 + [vmem] * 3,
        out_specs=(vmem,) * 3,
        scratch_shapes=[
            pltpu.VMEM((3, 2, cells, padded), F32),
            pltpu.VMEM((8, padded), F32),
            pltpu.VMEM((3, cells, padded), F32),
        ],
        name="slab",
    )(angle_ids, sides, place, density[0], attenuation[0], measured[:, 0])

    def regroup(blocks, count, width):
        if blocks.shape[0] == count:
            return blocks
        flat = blocks.transpose(1, 0, 2).reshape(blocks.shape[1], columns)
        return flat.reshape(blocks.shape[1], count, width).transpose(1, 0, 2)

    up = lax.all_to_all(regroup(up, devices, part), ("depth", "rows"), 0, 0)
    down = pl.pallas_call(
        functools.partial(column_kernel, views, slabs, rows),
        out_shape=jax.ShapeDtypeStruct(up.shape, F32),
        in_specs=[smem] * 2 + [vmem],
        out_specs=vmem,
        name="column",
    )(angle_ids, sides, up)
    down = regroup(lax.all_to_all(down, ("depth", "rows"), 0, 0), columns // wide, wide)
    grads = pl.pallas_call(
        functools.partial(gradient_kernel, views, wide),
        out_shape=(jax.ShapeDtypeStruct((cells, columns), F32),) * 2,
        in_specs=[smem] + [vmem] * 3,
        out_specs=(vmem,) * 2,
        scratch_shapes=[pltpu.VMEM((2, 3, cells, padded), F32)],
        name="gradient",
    )(angle_ids, down, light, behind)
    return grads[0][None], grads[1][None]


def solution(mesh):
    placed = (P("rows", "depth", None), P("rows", "depth", None), P(None, "rows", None), P(), P())
    return jax.shard_map(
        on_device,
        mesh=mesh,
        in_specs=placed,
        out_specs=(P("rows", "depth", None), P("rows", "depth", None)),
        check_vma=False,
    )
```

```python
import functools
import math

import jax
import jax.numpy as jnp
from jax import lax
from jax.experimental import pallas as pl
from jax.experimental.pallas import tpu as pltpu
from jax.sharding import PartitionSpec as P

ANGLES = 360
LANES, SUBS = 128, 8
GROUP = SUBS * SUBS
F32 = jnp.float32


def tilt_parts(angle):
    tilt = 0.8 * jnp.sin(jnp.pi * (angle.astype(F32) + 0.5) / ANGLES - jnp.pi / 2)
    return 1.0 - jnp.abs(tilt), jnp.maximum(tilt, 0.0), jnp.maximum(-tilt, 0.0)


def leans_right(angle):
    return 2 * angle >= ANGLES


def view_column(ref, views, shape):
    rows = lax.broadcasted_iota(jnp.int32, shape, 0)
    out = jnp.full(shape, ref[0], jnp.int32)
    for v in range(1, views):
        out = jnp.where(rows == v, ref[v], out)
    return out


def shift_tools():
    lane = lax.broadcasted_iota(jnp.int32, (SUBS, LANES), 1)

    def before(rolled, rolled_previous):
        return jnp.where(lane == 0, rolled_previous, rolled)

    def after(rolled, rolled_next):
        return jnp.where(lane == LANES - 1, rolled_next, rolled)

    return before, after, lambda x: pltpu.roll(x, 1, 1), lambda x: pltpu.roll(x, LANES - 1, 1)


def slab_kernel(
    views, angle_hbm, side_hbm, d_hbm, a_hbm, m_hbm, up_ref, lt_ref, front_ref,
    angle_ref, side_ref, raw_ref, ax_ref, dx_ref, m_ref, sem, sem_raw,
):
    blocks, length = raw_ref.shape[1:3]
    groups = length // GROUP
    place = lax.rem(lax.axis_index("depth"), views)
    small = [
        pltpu.make_async_copy(angle_hbm, angle_ref, sem.at[0]),
        pltpu.make_async_copy(side_hbm, side_ref, sem.at[1]),
        pltpu.make_async_copy(m_hbm.at[place], m_ref, sem.at[2]),
    ]

    def fetch(g):
        part = pl.ds(pl.multiple_of(g * GROUP, GROUP), GROUP)
        return [
            pltpu.make_async_copy(hbm.at[:, part], raw_ref.at[f, :, part], sem_raw.at[f, g])
            for f, hbm in enumerate((a_hbm, d_hbm))
        ]

    for g in range(groups):
        for copy in fetch(g):
            copy.start()
    for copy in small:
        copy.start()
    before, after, roll_up, roll_down = shift_tools()
    scale = -math.log2(math.e)

    for copy in fetch(0):
        copy.wait()
    for copy in small:
        copy.wait()

    def shifts(g, carry):
        base = pl.multiple_of(g * GROUP, GROUP)
        ahead = jnp.minimum(g + 1, groups - 1)

        @pl.when(g + 1 < groups)
        def _():
            for copy in fetch(ahead):
                copy.wait()

        first, last = g == 0, g + 1 == groups
        starts = [pl.multiple_of(jnp.maximum(base - SUBS, 0), SUBS)]
        starts += [pl.multiple_of(base + SUBS * i, SUBS) for i in range(SUBS)]
        starts += [pl.multiple_of(jnp.minimum(base + GROUP, length - SUBS), SUBS)]
        totals = [None] * (SUBS + 2)
        for f in range(2):
            for b in range(blocks):
                tiles = [raw_ref[f, b, pl.ds(at, SUBS), :] for at in starts]
                if f == 0:
                    tiles = [scale * x for x in tiles]
                tiles[0] = jnp.where(first, 0.0, tiles[0])
                tiles[-1] = jnp.where(last, 0.0, tiles[-1])
                up = [roll_up(x) for x in tiles[:-1]]
                down = [roll_down(x) for x in tiles[1:]]
                for i in range(SUBS):
                    at = pl.ds(starts[i + 1], SUBS)
                    here = tiles[i + 1]
                    left = before(up[i + 1], up[i]) - here
                    right = after(down[i], down[i + 1]) - here
                    if f == 0:
                        ax_ref[0, b, at, :] = here
                        ax_ref[1, b, at, :] = left
                        ax_ref[2, b, at, :] = right
                    else:
                        dx_ref[0, b, at, :] = left
                        dx_ref[1, b, at, :] = right
                if f == 0:
                    totals = [x if y is None else x + y for x, y in zip(tiles, totals)]
        totals = [jnp.sum(x, axis=0, keepdims=True) + jnp.zeros((SUBS, LANES), F32) for x in totals]
        up = [roll_up(x) for x in totals[:-1]]
        down = [roll_down(x) for x in totals[1:]]
        for i in range(SUBS):
            left = before(up[i + 1], up[i])
            right = after(down[i], down[i + 1])
            for row, value in enumerate((left, totals[i + 1], right)):
                up_ref[pl.ds(starts[i + 1] + views + row, 1), :] = value[:1]
        return carry

    lax.fori_loop(0, groups, shifts, 0)

    weights = []
    for v in range(views):
        _, left, right = tilt_parts(jnp.full((SUBS, LANES), angle_ref[v], jnp.int32))
        weights.append(left + right)
    shift = [jnp.where(leans_right(angle_ref[v]), 0, 1) for v in range(views)]
    far = [side_ref[v] == 1 for v in range(views)]

    def rays(g, carry):
        base = pl.multiple_of(g * GROUP, GROUP)
        depth = [jnp.zeros((SUBS, LANES), F32)] * views
        front = [jnp.zeros((SUBS, LANES), F32)] * views
        for i in range(blocks * SUBS):
            for v in range(views):
                b = jnp.where(far[v], blocks - 1 - i // SUBS, i // SUBS)
                at = pl.ds(base + jnp.where(far[v], SUBS - 1 - i % SUBS, i % SUBS), SUBS, stride=SUBS)
                light = jnp.exp2(depth[v])
                depth[v] = depth[v] + (ax_ref[0, b, at, :] + weights[v] * ax_ref[1 + shift[v], b, at, :])
                emission = raw_ref[1, b, at, :] + weights[v] * dx_ref[shift[v], b, at, :]
                front[v] = front[v] + emission * light
                lt_ref[v, b, at, :] = light
                front_ref[v, b, at, :] = front[v]
        for v in range(views):
            up_ref[pl.ds(base + v, SUBS, stride=SUBS), :] = front[v]
        up_ref[pl.ds(base + views + 3, SUBS, stride=SUBS), :] = m_ref[pl.ds(pl.multiple_of(g * SUBS, SUBS), SUBS), :]
        return carry

    lax.fori_loop(0, groups, rays, 0)


def column_kernel(views, slabs, rows, angle_ref, side_ref, up_ref, down_ref):
    height, wide = up_ref.shape[1:]
    shape = (views, wide)
    centre, left, right = tilt_parts(view_column(angle_ref, views, shape))
    far = view_column(side_ref, views, shape) == 1

    def blur(values):
        out = []
        for r in range(rows):
            total = 0.5 * values[r]
            if r > 0:
                total = total + 0.25 * values[r - 1]
            if r + 1 < rows:
                total = total + 0.25 * values[r + 1]
            out.append(total)
        return out

    for half in range(0, height, SUBS):
        passes, behinds, signals = {}, {}, []
        for r in range(rows):
            absorbs, runs = [], []
            run = jnp.zeros(shape, F32)
            for k in range(slabs):
                block = up_ref[k * rows + r, half : half + SUBS]
                absorb = left * block[views : views + 1] + centre * block[views + 1 : views + 2] + right * block[views + 2 : views + 3]
                runs.append(run)
                absorbs.append(absorb)
                run = run + absorb
            ends, starts = [], []
            signal = jnp.zeros(shape, F32)
            for k in range(slabs):
                entering = jnp.where(far, run - runs[k] - absorbs[k], runs[k])
                passes[k, r] = jnp.exp2(entering)
                starts.append(signal)
                signal = signal + passes[k, r] * up_ref[k * rows + r, half : half + views]
                ends.append(signal)
            for k in range(slabs):
                behinds[k, r] = jnp.where(far, -ends[k], starts[k] - signal)
            signals.append(signal)
        residuals = []
        for r, value in enumerate(blur(signals)):
            seen = [up_ref[v * rows + r, half + views + 3 : half + views + 4] for v in range(views)]
            residuals.append(value - jnp.concatenate(seen, axis=0))
        for r, back in enumerate(blur(residuals)):
            for k in range(slabs):
                scaled = back * behinds[k, r]
                parts = [back * passes[k, r]]
                for weight in (centre, left, right):
                    parts.append(jnp.sum(weight * scaled, axis=0, keepdims=True))
                parts.append(jnp.zeros((1, wide), F32))
                down_ref[k * rows + r, half : half + SUBS] = jnp.concatenate(parts, axis=0)


def gradient_kernel(views, angle_hbm, down_ref, lt_ref, front_ref, gd_hbm, ga_hbm, angle_ref, p_ref, out_ref, sem, sem_out):
    blocks, length = out_ref.shape[1:3]
    groups = length // GROUP
    copy = pltpu.make_async_copy(angle_hbm, angle_ref, sem)
    copy.start()
    copy.wait()
    before, after, roll_up, roll_down = shift_tools()
    right_of = [leans_right(angle_ref[v]).astype(jnp.int32) for v in range(views)]
    count = sum(right_of)
    order = [0] * views
    seen = [jnp.int32(0), jnp.int32(0)]
    for v in range(views):
        place = jnp.where(right_of[v] == 1, seen[0], count + seen[1])
        seen = [seen[0] + right_of[v], seen[1] + 1 - right_of[v]]
        order = [jnp.where(place == p, v, order[p]) for p in range(views)]
    weights = []
    for p in range(views):
        centre, left, right = tilt_parts(jnp.full((SUBS, LANES), angle_ref[order[p]], jnp.int32))
        weights.append((centre, left + right))

    def send(g):
        part = pl.ds(pl.multiple_of(g * GROUP, GROUP), GROUP)
        return [
            pltpu.make_async_copy(out_ref.at[q, :, part], hbm.at[:, part], sem_out.at[q, g])
            for q, hbm in enumerate((gd_hbm, ga_hbm))
        ]

    def products(ahead):
        def body(t, carry):
            at = pl.multiple_of(t * SUBS, SUBS)
            row = lambda f: jnp.broadcast_to(down_ref[pl.ds(at + f, 1), :], (SUBS, LANES))
            scales = []
            for p in range(views):
                back = row(order[p])
                scales.append((weights[p][0] * back, weights[p][1] * back))
            extra = [row(views + i) for i in range(3)]
            here = pl.ds(at, SUBS)
            for b in range(blocks):
                density, absorb = [None] * 3, list(extra)
                for p in range(views):
                    light = lt_ref[order[p], b, here, :]
                    front = front_ref[order[p], b, here, :]
                    for i, scale in ((0, scales[p][0]), (1 if p < ahead else 2, scales[p][1])):
                        density[i] = scale * light if density[i] is None else density[i] + scale * light
                        absorb[i] = absorb[i] + scale * front
                for i in range(3):
                    p_ref[0, i, b, here, :] = jnp.zeros((SUBS, LANES), F32) if density[i] is None else density[i]
                    p_ref[1, i, b, here, :] = absorb[i]
            return carry

        lax.fori_loop(0, groups * SUBS, body, 0)

    for ahead in range(views + 1):
        @pl.when(count == ahead)
        def _():
            products(ahead)

    def shifts(g, carry):
        base = pl.multiple_of(g * GROUP, GROUP)
        first, last = g == 0, g + 1 == groups
        own = [pl.multiple_of(base + SUBS * i, SUBS) for i in range(SUBS)]
        previous = pl.multiple_of(jnp.maximum(base - SUBS, 0), SUBS)
        following = pl.multiple_of(jnp.minimum(base + GROUP, length - SUBS), SUBS)
        for q in range(2):
            for b in range(blocks):
                up = [p_ref[q, 2, b, pl.ds(at, SUBS), :] for at in [previous] + own]
                down = [p_ref[q, 1, b, pl.ds(at, SUBS), :] for at in own + [following]]
                up[0] = jnp.where(first, 0.0, up[0])
                down[-1] = jnp.where(last, 0.0, down[-1])
                up = [roll_up(x) for x in up]
                down = [roll_down(x) for x in down]
                for i in range(SUBS):
                    at = pl.ds(own[i], SUBS)
                    value = p_ref[q, 0, b, at, :] + before(up[i + 1], up[i]) + after(down[i], down[i + 1])
                    out_ref[q, b, at, :] = value
        for copy in send(g):
            copy.start()
        return carry

    lax.fori_loop(0, groups, shifts, 0)
    for g in range(groups):
        for copy in send(g):
            copy.wait()


def on_device(density, attenuation, measured, angle_ids, sides):
    cells, columns = density.shape[1:]
    views = measured.shape[0]
    slabs, rows = lax.axis_size("depth"), lax.axis_size("rows")
    devices = slabs * rows
    assert views + 4 == SUBS and slabs >= views and cells % SUBS == 0 and columns % (SUBS * LANES) == 0
    part = columns // devices
    blocks, tiles = cells // SUBS, columns // LANES
    length = tiles * SUBS
    smem = pl.BlockSpec(memory_space=pltpu.SMEM)
    vmem = pl.BlockSpec(memory_space=pltpu.VMEM)
    leave = pl.BlockSpec(memory_space=pl.ANY)

    def in_hbm(x):
        return pltpu.with_memory_space_constraint(x, pltpu.HBM)

    def tiled(x):
        return x.reshape(blocks, SUBS, tiles, LANES).transpose(0, 2, 1, 3).reshape(blocks, length, LANES)

    def untiled(x):
        return x.reshape(blocks, tiles, SUBS, LANES).transpose(0, 2, 1, 3).reshape(1, cells, columns)

    field = pltpu.VMEM((views, blocks, length, LANES), F32)
    up, light, front = pl.pallas_call(
        functools.partial(slab_kernel, views),
        out_shape=(pltpu.VMEM((length, LANES), F32), field, field),
        in_specs=[leave] * 5,
        out_specs=(vmem,) * 3,
        scratch_shapes=[
            pltpu.SMEM((views,), jnp.int32),
            pltpu.SMEM((views,), jnp.int32),
            pltpu.VMEM((2, blocks, length, LANES), F32),
            pltpu.VMEM((3, blocks, length, LANES), F32),
            pltpu.VMEM((2, blocks, length, LANES), F32),
            pltpu.VMEM((tiles, LANES), F32),
            pltpu.SemaphoreType.DMA((3,)),
            pltpu.SemaphoreType.DMA((2, tiles // SUBS)),
        ],
        compiler_params=pltpu.CompilerParams(vmem_limit_bytes=32 << 20),
        name="slab",
    )(in_hbm(angle_ids), in_hbm(sides), in_hbm(tiled(density[0])), in_hbm(tiled(attenuation[0])), in_hbm(measured.reshape(views, tiles, LANES)))

    def to_parts(x):
        if part % LANES == 0:
            return x.reshape(devices, part // LANES * SUBS, LANES)
        x = x.reshape(tiles, SUBS, LANES).transpose(1, 0, 2).reshape(SUBS, devices, part)
        return x.transpose(1, 0, 2)

    def from_parts(x):
        if part % LANES == 0:
            return x.reshape(length, LANES)
        x = x.transpose(1, 0, 2).reshape(SUBS, tiles, LANES)
        return x.transpose(1, 0, 2).reshape(length, LANES)

    up = lax.all_to_all(to_parts(up), ("depth", "rows"), 0, 0)
    down = pl.pallas_call(
        functools.partial(column_kernel, views, slabs, rows),
        out_shape=jax.ShapeDtypeStruct(up.shape, F32),
        in_specs=[smem] * 2 + [vmem],
        out_specs=vmem,
        compiler_params=pltpu.CompilerParams(vmem_limit_bytes=16 << 20),
        name="column",
    )(angle_ids, sides, up)
    down = from_parts(lax.all_to_all(down, ("depth", "rows"), 0, 0))
    grads = pl.pallas_call(
        functools.partial(gradient_kernel, views),
        out_shape=(pltpu.HBM((blocks, length, LANES), F32),) * 2,
        in_specs=[leave] + [vmem] * 3,
        out_specs=(leave,) * 2,
        scratch_shapes=[
            pltpu.SMEM((views,), jnp.int32),
            pltpu.VMEM((2, 3, blocks, length, LANES), F32),
            pltpu.VMEM((2, blocks, length, LANES), F32),
            pltpu.SemaphoreType.DMA,
            pltpu.SemaphoreType.DMA((2, tiles // SUBS)),
        ],
        compiler_params=pltpu.CompilerParams(vmem_limit_bytes=32 << 20),
        name="gradient",
    )(in_hbm(angle_ids), down, light, front)
    return untiled(grads[0]), untiled(grads[1])


def solution(mesh):
    placed = (P("rows", "depth", None), P("rows", "depth", None), P(None, "rows", None), P(), P())
    return jax.shard_map(
        on_device,
        mesh=mesh,
        in_specs=placed,
        out_specs=(P("rows", "depth", None), P("rows", "depth", None)),
        check_vma=False,
    )
```

```python
import functools
import math

import jax
import jax.numpy as jnp
from jax import lax
from jax.experimental import pallas as pl
from jax.experimental.pallas import tpu as pltpu
from jax.sharding import PartitionSpec as P

ANGLES = 360
LANES, SUBS = 128, 8
GROUP = SUBS * SUBS
TILE = (SUBS, LANES)
F32 = jnp.float32


def tilt_parts(angle):
    tilt = 0.8 * jnp.sin(jnp.pi * (angle.astype(F32) + 0.5) / ANGLES - jnp.pi / 2)
    return 1.0 - jnp.abs(tilt), jnp.maximum(tilt, 0.0), jnp.maximum(-tilt, 0.0)


def leans_right(angle):
    return 2 * angle >= ANGLES


def near_first(sides, views):
    order = [0] * views
    seen = [jnp.int32(0), jnp.int32(views // 2)]
    for v in range(views):
        far = (sides[v] == 1).astype(jnp.int32)
        place = jnp.where(far == 1, seen[1], seen[0])
        seen = [seen[0] + 1 - far, seen[1] + far]
        order = [jnp.where(place == p, v, order[p]) for p in range(views)]
    return order


def lanes():
    return lax.broadcasted_iota(jnp.int32, TILE, 1)


def subs():
    return lax.broadcasted_iota(jnp.int32, TILE, 0)


def spread(row):
    return jnp.broadcast_to(row, TILE)


def moved_right(blocks):
    first_lane, first_sub = lanes() == 0, subs() == 0
    out, carried = [], jnp.zeros(TILE, F32)
    for x in blocks:
        rolled = pltpu.roll(x, 1, 1)
        down = pltpu.roll(rolled, 1, 0)
        out.append(jnp.where(first_lane, jnp.where(first_sub, carried, down), rolled))
        carried = down
    return out


def moved_left(blocks):
    last_lane, last_sub = lanes() == LANES - 1, subs() == SUBS - 1
    out, carried = [], jnp.zeros(TILE, F32)
    for x in reversed(blocks):
        rolled = pltpu.roll(x, LANES - 1, 1)
        up = pltpu.roll(rolled, SUBS - 1, 0)
        out.append(jnp.where(last_lane, jnp.where(last_sub, carried, up), rolled))
        carried = up
    return out[::-1]


def slab_kernel(
    views, slabs, angle_hbm, side_hbm, d_hbm, a_hbm, m_hbm, up_ref, tilt_ref, field_ref,
    angle_ref, side_ref, raw_ref, ax_ref, dx_ref, sum_ref, m_ref, sem, sem_raw,
):
    blocks, length = raw_ref.shape[1:3]
    cells, groups, fields = blocks * SUBS, length // GROUP, views + 2
    slab = lax.axis_index("depth")
    share = max(slabs // views, 1)

    def fetch(b):
        return [pltpu.make_async_copy(hbm.at[b], raw_ref.at[f, b], sem_raw.at[f, b]) for f, hbm in enumerate((a_hbm, d_hbm))]

    small = [pltpu.make_async_copy(angle_hbm, angle_ref, sem.at[0]), pltpu.make_async_copy(side_hbm, side_ref, sem.at[1])]
    for copy in small + [copy for b in range(blocks) for copy in fetch(b)]:
        copy.start()
    for copy in small:
        copy.wait()
    order = near_first(side_ref, views)
    seen = jnp.int32(0)
    for p in range(views):
        seen = jnp.where(lax.rem(slab // share, views) == p, order[p], seen)
    fetch_m = pltpu.make_async_copy(m_hbm.at[seen], m_ref, sem.at[2])
    fetch_m.start()
    angle_block = jnp.zeros(TILE, jnp.int32)
    for p in range(views):
        angle_block = jnp.where(subs() == p, angle_ref[order[p]], angle_block)
    parts = tilt_parts(angle_block)
    for i, part in enumerate(parts):
        tilt_ref[i] = part
    beside = parts[1] + parts[2]
    weights = [spread(beside[p : p + 1]) for p in range(views)]
    shift = [jnp.where(leans_right(angle_ref[order[p]]), 0, 1) for p in range(views)]
    scale = -math.log2(math.e)
    sum_ref[...] = jnp.zeros(sum_ref.shape, F32)

    def shifts(z, carry):
        b = z // SUBS
        row = lax.rem(z, SUBS)

        @pl.when(row == 0)
        def _():
            for copy in fetch(b):
                copy.wait()

        absorbs = [scale * raw_ref[0, b, pl.ds(g * GROUP + row, SUBS, stride=SUBS), :] for g in range(groups)]
        for g, (here, left, right) in enumerate(zip(absorbs, moved_right(absorbs), moved_left(absorbs))):
            ax_ref[0, z, g] = here
            ax_ref[1, z, g] = left - here
            ax_ref[2, z, g] = right - here
            sum_ref[g] = sum_ref[g] + here
        density = [raw_ref[1, b, pl.ds(g * GROUP + row, SUBS, stride=SUBS), :] for g in range(groups)]
        for g, (here, left, right) in enumerate(zip(density, moved_right(density), moved_left(density))):
            dx_ref[0, z, g] = here
            dx_ref[1, z, g] = left - here
            dx_ref[2, z, g] = right - here
        return carry

    lax.fori_loop(0, cells, shifts, 0)

    def put(g, field, value):
        up_ref[pl.ds(g * SUBS * fields + field, SUBS, stride=fields), :] = value

    def rays(g, carry):
        depth = [jnp.zeros(TILE, F32)] * views
        front = [jnp.zeros(TILE, F32)] * views
        for i in range(cells):
            for p in range(views):
                z = i if p < views // 2 else cells - 1 - i
                light = jnp.exp2(depth[p])
                depth[p] = depth[p] + (ax_ref[0, z, g] + weights[p] * ax_ref[1 + shift[p], z, g])
                front[p] = front[p] + (dx_ref[0, z, g] + weights[p] * dx_ref[1 + shift[p], z, g]) * light
                field_ref[0, p, z, g] = light
                field_ref[1, p, z, g] = front[p]
        for p in range(views):
            put(g, p, front[p])
        return carry

    lax.fori_loop(0, groups, rays, 0)
    fetch_m.wait()
    totals = [sum_ref[g] for g in range(groups)]
    odd = lax.rem(subs(), 2) == 1
    second = lax.rem(slab, share) == 1
    for g, (before, after) in enumerate(zip(moved_right(totals), moved_left(totals))):
        counts = m_ref[pl.ds(g * SUBS, SUBS), :]
        counts = jnp.where(second, pltpu.roll(counts, SUBS - 1, 0), counts)
        edges = jnp.where(lanes() == 0, pltpu.roll(before, 1, 0), after)
        put(g, views, totals[g])
        put(g, views + 1, jnp.where(odd, edges, counts))


def blur(values):
    out = []
    for r in range(len(values)):
        total = 0.5 * values[r]
        if r > 0:
            total = total + 0.25 * values[r - 1]
        if r + 1 < len(values):
            total = total + 0.25 * values[r + 1]
        out.append(total)
    return out


def column_kernel(views, rows, tilt_ref, up_ref, down_ref):
    fields = views + 2
    record = 2 * fields
    first_lane, last_lane, sub = lanes() == 0, lanes() == LANES - 1, subs()
    weights = [[spread(tilt_ref[i, p : p + 1]) for i in range(3)] for p in range(views)]

    def get(r, half, field):
        return up_ref[pl.ds(r * record + half * fields + field, SUBS, stride=rows * record), :]

    def put(r, half, field, value):
        down_ref[pl.ds(r * record + half * fields + field, SUBS, stride=rows * record), :] = value

    def scan(value, far):
        step = 1
        while step < SUBS:
            if far:
                value = value + jnp.where(sub >= step, pltpu.roll(value, step, 0), 0.0)
            else:
                value = value + jnp.where(sub < SUBS - step, pltpu.roll(value, SUBS - step, 0), 0.0)
            step *= 2
        return value

    passes, behinds = {}, {}
    signals = {(p, half): [] for p in range(views) for half in range(2)}
    for r in range(rows):
        total = [get(r, half, views) for half in range(2)]
        edges = get(r, 1, views + 1)
        up = [pltpu.roll(x, 1, 1) for x in total]
        down = [pltpu.roll(x, LANES - 1, 1) for x in total]
        before = [jnp.where(first_lane, edges, up[0]), jnp.where(first_lane, up[0], up[1])]
        after = [jnp.where(last_lane, down[1], down[0]), jnp.where(last_lane, edges, down[1])]
        for half in range(2):
            for p in range(views):
                far = p >= views // 2
                centre, left, right = weights[p]
                absorb = centre * total[half] + left * before[half] + right * after[half]
                entering = scan(absorb, not far) - absorb
                light = jnp.exp2(entering)
                behind = scan(light * get(r, half, p), far)
                passes[r, half, p] = light
                behinds[r, half, p] = behind
                edge = SUBS - 1 if far else 0
                signals[p, half].append(spread(behind[edge : edge + 1]))
    backs = {}
    for p in range(views):
        for half in range(2):
            residuals = []
            for r, value in enumerate(blur(signals[p, half])):
                at = ((p * (SUBS // views) + half) * rows + r) * record + views + 1
                residuals.append(value - spread(up_ref[pl.ds(at, 1), :]))
            backs[p, half] = blur(residuals)
    for r in range(rows):
        sums = []
        for half in range(2):
            parts = [jnp.zeros(TILE, F32)] * 3
            for p in range(views):
                back = backs[p, half][r]
                put(r, half, p, back * passes[r, half, p])
                scaled = back * behinds[r, half, p]
                parts = [part - weight * scaled for part, weight in zip(parts, weights[p])]
            sums.append(parts)
        next_up = [pltpu.roll(sums[half][1], LANES - 1, 1) for half in range(2)]
        previous = [pltpu.roll(sums[half][2], 1, 1) for half in range(2)]
        zero = jnp.zeros(TILE, F32)
        put(r, 0, views, sums[0][0] + jnp.where(last_lane, next_up[1], next_up[0]) + jnp.where(first_lane, zero, previous[0]))
        put(r, 1, views, sums[1][0] + jnp.where(last_lane, zero, next_up[1]) + jnp.where(first_lane, previous[0], previous[1]))
        put(r, 0, views + 1, jnp.where(last_lane, next_up[0], zero))
        put(r, 1, views + 1, jnp.where(first_lane, previous[1], zero))


def wide_column_kernel(views, slabs, rows, tilt_ref, up_ref, down_ref):
    wide = up_ref.shape[2]
    shape = (views, wide)
    centre, left, right = [tilt_ref[i, :views, :1] for i in range(3)]
    far = lax.broadcasted_iota(jnp.int32, shape, 0) >= views // 2
    passes, behinds, signals = {}, {}, []
    for r in range(rows):
        absorbs, runs = [], []
        run = jnp.zeros(shape, F32)
        for k in range(slabs):
            block = up_ref[k * rows + r]
            absorb = left * block[views : views + 1] + centre * block[views + 1 : views + 2] + right * block[views + 2 : views + 3]
            runs.append(run)
            absorbs.append(absorb)
            run = run + absorb
        ends, starts = [], []
        signal = jnp.zeros(shape, F32)
        for k in range(slabs):
            entering = jnp.where(far, run - runs[k] - absorbs[k], runs[k])
            passes[k, r] = jnp.exp2(entering)
            starts.append(signal)
            signal = signal + passes[k, r] * up_ref[k * rows + r, :views]
            ends.append(signal)
        for k in range(slabs):
            behinds[k, r] = jnp.where(far, -ends[k], starts[k] - signal)
        signals.append(signal)
    residuals = []
    for r, value in enumerate(blur(signals)):
        seen = [up_ref[(v * max(slabs // views, 1)) * rows + r, views + 3 : views + 4] for v in range(views)]
        residuals.append(value - jnp.concatenate(seen, axis=0))
    for r, back in enumerate(blur(residuals)):
        for k in range(slabs):
            scaled = back * behinds[k, r]
            parts = [back * passes[k, r]]
            for weight in (centre, left, right):
                parts.append(jnp.sum(weight * scaled, axis=0, keepdims=True))
            parts.append(jnp.zeros((1, wide), F32))
            down_ref[k * rows + r] = jnp.concatenate(parts, axis=0)


def gradient_kernel(views, tilt_ref, down_ref, field_ref, gd_hbm, ga_hbm, scale_ref, out_ref, sem_out):
    cells, groups = field_ref.shape[2:4]
    fields = views + 2

    def send(b):
        return [pltpu.make_async_copy(out_ref.at[q, b], hbm.at[b], sem_out.at[q, b]) for q, hbm in enumerate((gd_hbm, ga_hbm))]

    def get(g, field):
        return down_ref[pl.ds(g * SUBS * fields + field, SUBS, stride=fields), :]

    for p in range(views):
        centre, left, right = [spread(tilt_ref[i, p : p + 1]) for i in range(3)]
        for g in range(groups):
            back = get(g, p)
            scale_ref[0, p, g] = centre * back
            scale_ref[1, p, g] = (left + right) * back
    odd = lax.rem(subs(), 2) == 1
    extras = [get(g, views + 1) for g in range(groups)]
    zero = jnp.zeros(TILE, F32)
    for g in range(groups):
        later = pltpu.roll(extras[g], SUBS - 1, 0)
        ahead = pltpu.roll(extras[g + 1], SUBS - 1, 0) if g + 1 < groups else zero
        later = jnp.where(subs() == SUBS - 1, ahead, later)
        earlier = pltpu.roll(extras[g], 1, 0)
        past = pltpu.roll(extras[g - 1], 1, 0) if g > 0 else zero
        earlier = jnp.where(subs() == 0, past, earlier)
        scale_ref[2, 0, g] = get(g, views) + jnp.where(odd, later, earlier)

    right_of = [(tilt_ref[1, p, 0] > 0.0).astype(jnp.int32) for p in range(views)]
    count = sum(right_of)
    order = [0] * views
    seen = [jnp.int32(0), count]
    for v in range(views):
        place = jnp.where(right_of[v] == 1, seen[0], seen[1])
        seen = [seen[0] + right_of[v], seen[1] + 1 - right_of[v]]
        order = [jnp.where(place == p, v, order[p]) for p in range(views)]

    def products(ahead):
        def body(z, carry):
            b, row = z // SUBS, lax.rem(z, SUBS)
            sums = [[], [], [], [], [], []]
            for g in range(groups):
                for q in range(2):
                    parts = [scale_ref[2, 0, g] if q == 1 else None, None, None]
                    for p in range(views):
                        value = field_ref[q, order[p], z, g]
                        for i, scale in ((0, scale_ref[0, order[p], g]), (1 if p < ahead else 2, scale_ref[1, order[p], g])):
                            parts[i] = scale * value if parts[i] is None else parts[i] + scale * value
                    for i in range(3):
                        sums[3 * q + i].append(parts[i])
            for q in range(2):
                total = sums[3 * q]
                if ahead > 0:
                    total = [x + y for x, y in zip(total, moved_left(sums[3 * q + 1]))]
                if ahead < views:
                    total = [x + y for x, y in zip(total, moved_right(sums[3 * q + 2]))]
                for g in range(groups):
                    out_ref[q, b, pl.ds(g * GROUP + row, SUBS, stride=SUBS), :] = total[g]

            @pl.when(row == SUBS - 1)
            def _():
                for copy in send(b):
                    copy.start()

            return carry

        lax.fori_loop(0, cells, body, 0)

    for ahead in range(views + 1):

        @pl.when(count == ahead)
        def _():
            products(ahead)

    for b in range(cells // SUBS):
        for copy in send(b):
            copy.wait()


def on_device(density, attenuation, measured, angle_ids, sides):
    cells, columns = density.shape[1:]
    views = measured.shape[0]
    slabs, rows = lax.axis_size("depth"), lax.axis_size("rows")
    devices = slabs * rows
    assert views == 4 and slabs % views == 0 and cells % SUBS == 0 and columns % (SUBS * LANES) == 0
    part = columns // devices
    compact = slabs == SUBS and part == 2 * LANES
    blocks, tiles = cells // SUBS, columns // LANES
    groups, length, fields = tiles // SUBS, tiles * SUBS, views + 2
    vmem = pl.BlockSpec(memory_space=pltpu.VMEM)
    leave = pl.BlockSpec(memory_space=pl.ANY)

    def grant(mib):
        return pltpu.CompilerParams(vmem_limit_bytes=mib << 20)

    def in_hbm(x):
        return pltpu.with_memory_space_constraint(x, pltpu.HBM)

    def tiled(x):
        return x.reshape(blocks, SUBS, tiles, LANES).transpose(0, 2, 1, 3).reshape(blocks, length, LANES)

    def untiled(x):
        return x.reshape(blocks, tiles, SUBS, LANES).transpose(0, 2, 1, 3).reshape(1, cells, columns)

    ids_in = [in_hbm(angle_ids), in_hbm(sides)]
    ids = [pltpu.SMEM((views,), jnp.int32)] * 2
    field = pltpu.VMEM((2, views, cells, groups) + TILE, F32)
    shifted = pltpu.VMEM((3, cells, groups, SUBS, LANES), F32)
    up, tilts, light = pl.pallas_call(
        functools.partial(slab_kernel, views, slabs),
        out_shape=(pltpu.VMEM((tiles * fields, LANES), F32), pltpu.VMEM((3,) + TILE, F32), field),
        in_specs=[leave] * 5,
        out_specs=(vmem,) * 3,
        scratch_shapes=ids
        + [
            pltpu.VMEM((2, blocks, length, LANES), F32),
            shifted,
            shifted,
            pltpu.VMEM((groups,) + TILE, F32),
            pltpu.VMEM((tiles, LANES), F32),
            pltpu.SemaphoreType.DMA((3,)),
            pltpu.SemaphoreType.DMA((2, blocks)),
        ],
        compiler_params=grant(24),
        name="slab",
    )(
        *ids_in,
        in_hbm(tiled(density[0])),
        in_hbm(tiled(attenuation[0])),
        in_hbm(measured.reshape(views, tiles, LANES)),
    )

    def exchange(x):
        return lax.all_to_all(x, ("depth", "rows"), 0, 0, tiled=True)

    if compact:
        rows_of = (devices * 2 * fields // 4, 4, LANES)
        up = exchange(up.reshape(rows_of)).reshape(tiles * fields, LANES)
    else:
        flat = up.reshape(tiles, fields, LANES).transpose(1, 0, 2).reshape(fields, columns)
        total = flat[views : views + 1]
        order = jnp.argsort(sides, stable=True)
        place = lax.rem(lax.axis_index("depth") // (slabs // views), views)
        counts = lax.dynamic_index_in_dim(measured[:, 0], order[place], 0)
        before = jnp.pad(total[:, :-1], ((0, 0), (1, 0)))
        after = jnp.pad(total[:, 1:], ((0, 0), (0, 1)))
        flat = jnp.concatenate([flat[:views], before, total, after, counts], axis=0)
        up = exchange(flat.reshape(SUBS, devices, part).transpose(1, 0, 2))
    kernel = functools.partial(column_kernel, views, rows) if compact else functools.partial(wide_column_kernel, views, slabs, rows)
    down = pl.pallas_call(
        kernel,
        out_shape=pltpu.VMEM(up.shape, F32) if compact else jax.ShapeDtypeStruct(up.shape, F32),
        in_specs=[vmem] * 2,
        out_specs=vmem,
        compiler_params=grant(4 if compact else 16),
        name="column",
    )(tilts, up)
    if compact:
        down = exchange(down.reshape(rows_of)).reshape(tiles * fields, LANES)
    else:
        flat = exchange(down).transpose(1, 0, 2).reshape(SUBS, columns)
        base = flat[views] + jnp.pad(flat[views + 1, 1:], (0, 1)) + jnp.pad(flat[views + 2, :-1], (1, 0))
        flat = jnp.concatenate([flat[:views], base[None], jnp.zeros((1, columns), F32)], axis=0)
        down = flat.reshape(fields, tiles, LANES).transpose(1, 0, 2).reshape(tiles * fields, LANES)
    grads = pl.pallas_call(
        functools.partial(gradient_kernel, views),
        out_shape=(pltpu.HBM((blocks, length, LANES), F32),) * 2,
        in_specs=[vmem] * 3,
        out_specs=(leave,) * 2,
        scratch_shapes=[
            pltpu.VMEM((3, views, groups) + TILE, F32),
            pltpu.VMEM((2, blocks, length, LANES), F32),
            pltpu.SemaphoreType.DMA((2, blocks)),
        ],
        compiler_params=grant(8),
        name="gradient",
    )(tilts, down, light)
    return untiled(grads[0]), untiled(grads[1])


def solution(mesh):
    placed = (P("rows", "depth", None), P("rows", "depth", None), P(None, "rows", None), P(), P())
    return jax.shard_map(
        on_device,
        mesh=mesh,
        in_specs=placed,
        out_specs=(P("rows", "depth", None), P("rows", "depth", None)),
        check_vma=False,
    )
```

```python
import functools
import math

import jax
import jax.numpy as jnp
from jax import lax
from jax.experimental import pallas as pl
from jax.experimental.pallas import tpu as pltpu
from jax.sharding import PartitionSpec as P

ANGLES = 360
LANES, SUBS = 128, 8
GROUP = SUBS * SUBS
TILE = (SUBS, LANES)
F32 = jnp.float32


def tilt_parts(angle):
    tilt = 0.8 * jnp.sin(jnp.pi * (angle.astype(F32) + 0.5) / ANGLES - jnp.pi / 2)
    return 1.0 - jnp.abs(tilt), jnp.maximum(tilt, 0.0), jnp.maximum(-tilt, 0.0)


def leans_right(angle):
    return 2 * angle >= ANGLES


def near_first(sides, views):
    order = [0] * views
    seen = [jnp.int32(0), jnp.int32(views // 2)]
    for v in range(views):
        far = (sides[v] == 1).astype(jnp.int32)
        place = jnp.where(far == 1, seen[1], seen[0])
        seen = [seen[0] + 1 - far, seen[1] + far]
        order = [jnp.where(place == p, v, order[p]) for p in range(views)]
    return order


def lanes():
    return lax.broadcasted_iota(jnp.int32, TILE, 1)


def subs():
    return lax.broadcasted_iota(jnp.int32, TILE, 0)


def spread(row):
    return jnp.broadcast_to(row, TILE)


def moved_right(blocks):
    first_lane, first_sub = lanes() == 0, subs() == 0
    out, carried = [], jnp.zeros(TILE, F32)
    for x in blocks:
        rolled = pltpu.roll(x, 1, 1)
        down = pltpu.roll(rolled, 1, 0)
        out.append(jnp.where(first_lane, jnp.where(first_sub, carried, down), rolled))
        carried = down
    return out


def moved_left(blocks):
    last_lane, last_sub = lanes() == LANES - 1, subs() == SUBS - 1
    out, carried = [], jnp.zeros(TILE, F32)
    for x in reversed(blocks):
        rolled = pltpu.roll(x, LANES - 1, 1)
        up = pltpu.roll(rolled, SUBS - 1, 0)
        out.append(jnp.where(last_lane, jnp.where(last_sub, carried, up), rolled))
        carried = up
    return out[::-1]


def slab_kernel(
    views, slabs, angle_hbm, side_hbm, d_hbm, a_hbm, m_hbm, up_ref, tilt_ref, field_ref,
    angle_ref, side_ref, raw_ref, ax_ref, dx_ref, sum_ref, m_ref, sem, sem_raw,
):
    blocks, length = raw_ref.shape[1:3]
    cells, groups, fields = blocks * SUBS, length // GROUP, views + 2
    slab = lax.axis_index("depth")
    share = max(slabs // views, 1)

    def fetch(b):
        return [pltpu.make_async_copy(hbm.at[b], raw_ref.at[f, b], sem_raw.at[f, b]) for f, hbm in enumerate((a_hbm, d_hbm))]

    small = [pltpu.make_async_copy(angle_hbm, angle_ref, sem.at[0]), pltpu.make_async_copy(side_hbm, side_ref, sem.at[1])]
    for copy in small + [copy for b in range(blocks) for copy in fetch(b)]:
        copy.start()
    scale = -math.log2(math.e)
    sum_ref[...] = jnp.zeros(sum_ref.shape, F32)

    steps = 8

    def shifts(i, carry):
        b = i // (SUBS // steps)
        first = lax.rem(i, SUBS // steps)

        @pl.when(first == 0)
        def _():
            for copy in fetch(b):
                copy.wait()

        sums = [sum_ref[g] for g in range(groups)]
        for step in range(steps):
            z, row = i * steps + step, first * steps + step
            for f, ref in enumerate((ax_ref, dx_ref)):
                values = [raw_ref[f, b, pl.ds(g * GROUP + row, SUBS, stride=SUBS), :] for g in range(groups)]
                if f == 0:
                    values = [scale * x for x in values]
                    sums = [x + y for x, y in zip(sums, values)]
                for g, (here, left, right) in enumerate(zip(values, moved_right(values), moved_left(values))):
                    ref[0, z, g] = here
                    ref[1, z, g] = left - here
                    ref[2, z, g] = right - here
        for g in range(groups):
            sum_ref[g] = sums[g]
        return carry

    lax.fori_loop(0, cells // steps, shifts, 0)
    for copy in small:
        copy.wait()
    order = near_first(side_ref, views)
    seen = jnp.int32(0)
    for p in range(views):
        seen = jnp.where(lax.rem(slab // share, views) == p, order[p], seen)
    fetch_m = pltpu.make_async_copy(m_hbm.at[seen], m_ref, sem.at[2])
    fetch_m.start()
    angle_block = jnp.zeros(TILE, jnp.int32)
    for p in range(views):
        angle_block = jnp.where(subs() == p, angle_ref[order[p]], angle_block)
    parts = tilt_parts(angle_block)
    for i, part in enumerate(parts):
        tilt_ref[i] = part
    beside = parts[1] + parts[2]
    weights = [spread(beside[p : p + 1]) for p in range(views)]
    shift = [jnp.where(leans_right(angle_ref[order[p]]), 0, 1) for p in range(views)]

    def put(g, field, value):
        up_ref[pl.ds(g * SUBS * fields + field, SUBS, stride=fields), :] = value

    abreast = 2

    def rays(i, carry):
        several = [i * abreast + j for j in range(abreast)]
        depth = {(j, p): jnp.zeros(TILE, F32) for j in range(abreast) for p in range(views)}
        front = dict(depth)
        for i in range(cells):
            for j, g in enumerate(several):
                for p in range(views):
                    z = i if p < views // 2 else cells - 1 - i
                    light = jnp.exp2(depth[j, p])
                    depth[j, p] = depth[j, p] + (ax_ref[0, z, g] + weights[p] * ax_ref[1 + shift[p], z, g])
                    front[j, p] = front[j, p] + (dx_ref[0, z, g] + weights[p] * dx_ref[1 + shift[p], z, g]) * light
                    field_ref[0, p, z, g] = light
                    field_ref[1, p, z, g] = front[j, p]
        for j, g in enumerate(several):
            for p in range(views):
                put(g, p, front[j, p])
        return carry

    lax.fori_loop(0, groups // abreast, rays, 0)
    fetch_m.wait()
    totals = [sum_ref[g] for g in range(groups)]
    odd = lax.rem(subs(), 2) == 1
    second = lax.rem(slab, share) == 1
    for g, (before, after) in enumerate(zip(moved_right(totals), moved_left(totals))):
        counts = m_ref[pl.ds(g * SUBS, SUBS), :]
        counts = jnp.where(second, pltpu.roll(counts, SUBS - 1, 0), counts)
        edges = jnp.where(lanes() == 0, pltpu.roll(before, 1, 0), after)
        put(g, views, totals[g])
        put(g, views + 1, jnp.where(odd, edges, counts))


def blur(values):
    out = []
    for r in range(len(values)):
        total = 0.5 * values[r]
        if r > 0:
            total = total + 0.25 * values[r - 1]
        if r + 1 < len(values):
            total = total + 0.25 * values[r + 1]
        out.append(total)
    return out


def column_kernel(views, rows, tilt_ref, up_ref, down_ref):
    fields = views + 2
    record = 2 * fields
    first_lane, last_lane, sub = lanes() == 0, lanes() == LANES - 1, subs()
    weights = [[spread(tilt_ref[i, p : p + 1]) for i in range(3)] for p in range(views)]

    def get(r, half, field):
        return up_ref[pl.ds(r * record + half * fields + field, SUBS, stride=rows * record), :]

    def put(r, half, field, value):
        down_ref[pl.ds(r * record + half * fields + field, SUBS, stride=rows * record), :] = value

    def scan(value, far):
        step = 1
        while step < SUBS:
            if far:
                value = value + jnp.where(sub >= step, pltpu.roll(value, step, 0), 0.0)
            else:
                value = value + jnp.where(sub < SUBS - step, pltpu.roll(value, SUBS - step, 0), 0.0)
            step *= 2
        return value

    passes, behinds = {}, {}
    signals = {(p, half): [] for p in range(views) for half in range(2)}
    for r in range(rows):
        total = [get(r, half, views) for half in range(2)]
        edges = get(r, 1, views + 1)
        up = [pltpu.roll(x, 1, 1) for x in total]
        down = [pltpu.roll(x, LANES - 1, 1) for x in total]
        before = [jnp.where(first_lane, edges, up[0]), jnp.where(first_lane, up[0], up[1])]
        after = [jnp.where(last_lane, down[1], down[0]), jnp.where(last_lane, edges, down[1])]
        for half in range(2):
            for p in range(views):
                far = p >= views // 2
                centre, left, right = weights[p]
                absorb = centre * total[half] + left * before[half] + right * after[half]
                entering = scan(absorb, not far) - absorb
                light = jnp.exp2(entering)
                behind = scan(light * get(r, half, p), far)
                passes[r, half, p] = light
                behinds[r, half, p] = behind
                edge = SUBS - 1 if far else 0
                signals[p, half].append(spread(behind[edge : edge + 1]))
    backs = {}
    for p in range(views):
        for half in range(2):
            residuals = []
            for r, value in enumerate(blur(signals[p, half])):
                at = ((p * (SUBS // views) + half) * rows + r) * record + views + 1
                residuals.append(value - spread(up_ref[pl.ds(at, 1), :]))
            backs[p, half] = blur(residuals)
    for r in range(rows):
        sums = []
        for half in range(2):
            parts = [jnp.zeros(TILE, F32)] * 3
            for p in range(views):
                back = backs[p, half][r]
                put(r, half, p, back * passes[r, half, p])
                scaled = back * behinds[r, half, p]
                parts = [part - weight * scaled for part, weight in zip(parts, weights[p])]
            sums.append(parts)
        next_up = [pltpu.roll(sums[half][1], LANES - 1, 1) for half in range(2)]
        previous = [pltpu.roll(sums[half][2], 1, 1) for half in range(2)]
        zero = jnp.zeros(TILE, F32)
        put(r, 0, views, sums[0][0] + jnp.where(last_lane, next_up[1], next_up[0]) + jnp.where(first_lane, zero, previous[0]))
        put(r, 1, views, sums[1][0] + jnp.where(last_lane, zero, next_up[1]) + jnp.where(first_lane, previous[0], previous[1]))
        put(r, 0, views + 1, jnp.where(last_lane, next_up[0], zero))
        put(r, 1, views + 1, jnp.where(first_lane, previous[1], zero))


def wide_column_kernel(views, slabs, rows, tilt_ref, up_ref, down_ref):
    wide = up_ref.shape[2]
    shape = (views, wide)
    centre, left, right = [tilt_ref[i, :views, :1] for i in range(3)]
    far = lax.broadcasted_iota(jnp.int32, shape, 0) >= views // 2
    passes, behinds, signals = {}, {}, []
    for r in range(rows):
        absorbs, runs = [], []
        run = jnp.zeros(shape, F32)
        for k in range(slabs):
            block = up_ref[k * rows + r]
            absorb = left * block[views : views + 1] + centre * block[views + 1 : views + 2] + right * block[views + 2 : views + 3]
            runs.append(run)
            absorbs.append(absorb)
            run = run + absorb
        ends, starts = [], []
        signal = jnp.zeros(shape, F32)
        for k in range(slabs):
            entering = jnp.where(far, run - runs[k] - absorbs[k], runs[k])
            passes[k, r] = jnp.exp2(entering)
            starts.append(signal)
            signal = signal + passes[k, r] * up_ref[k * rows + r, :views]
            ends.append(signal)
        for k in range(slabs):
            behinds[k, r] = jnp.where(far, -ends[k], starts[k] - signal)
        signals.append(signal)
    residuals = []
    for r, value in enumerate(blur(signals)):
        seen = [up_ref[(v * max(slabs // views, 1)) * rows + r, views + 3 : views + 4] for v in range(views)]
        residuals.append(value - jnp.concatenate(seen, axis=0))
    for r, back in enumerate(blur(residuals)):
        for k in range(slabs):
            scaled = back * behinds[k, r]
            parts = [back * passes[k, r]]
            for weight in (centre, left, right):
                parts.append(jnp.sum(weight * scaled, axis=0, keepdims=True))
            parts.append(jnp.zeros((1, wide), F32))
            down_ref[k * rows + r] = jnp.concatenate(parts, axis=0)


def gradient_kernel(views, tilt_ref, down_ref, field_ref, gd_hbm, ga_hbm, scale_ref, out_ref, sem_out):
    cells, groups = field_ref.shape[2:4]
    fields = views + 2

    def send(b):
        return [pltpu.make_async_copy(out_ref.at[q, b], hbm.at[b], sem_out.at[q, b]) for q, hbm in enumerate((gd_hbm, ga_hbm))]

    def get(g, field):
        return down_ref[pl.ds(g * SUBS * fields + field, SUBS, stride=fields), :]

    for p in range(views):
        centre, left, right = [spread(tilt_ref[i, p : p + 1]) for i in range(3)]
        for g in range(groups):
            back = get(g, p)
            scale_ref[0, p, g] = centre * back
            scale_ref[1, p, g] = (left + right) * back
    odd = lax.rem(subs(), 2) == 1
    extras = [get(g, views + 1) for g in range(groups)]
    zero = jnp.zeros(TILE, F32)
    for g in range(groups):
        later = pltpu.roll(extras[g], SUBS - 1, 0)
        ahead = pltpu.roll(extras[g + 1], SUBS - 1, 0) if g + 1 < groups else zero
        later = jnp.where(subs() == SUBS - 1, ahead, later)
        earlier = pltpu.roll(extras[g], 1, 0)
        past = pltpu.roll(extras[g - 1], 1, 0) if g > 0 else zero
        earlier = jnp.where(subs() == 0, past, earlier)
        scale_ref[2, 0, g] = get(g, views) + jnp.where(odd, later, earlier)

    right_of = [(tilt_ref[1, p, 0] > 0.0).astype(jnp.int32) for p in range(views)]
    count = sum(right_of)
    order = [0] * views
    seen = [jnp.int32(0), count]
    for v in range(views):
        place = jnp.where(right_of[v] == 1, seen[0], seen[1])
        seen = [seen[0] + right_of[v], seen[1] + 1 - right_of[v]]
        order = [jnp.where(place == p, v, order[p]) for p in range(views)]

    def products(ahead):
        steps = 4

        def cell(z, b, row):
            sums = [[], [], [], [], [], []]
            for g in range(groups):
                for q in range(2):
                    parts = [scale_ref[2, 0, g] if q == 1 else None, None, None]
                    for p in range(views):
                        value = field_ref[q, order[p], z, g]
                        for i, scale in ((0, scale_ref[0, order[p], g]), (1 if p < ahead else 2, scale_ref[1, order[p], g])):
                            parts[i] = scale * value if parts[i] is None else parts[i] + scale * value
                    for i in range(3):
                        sums[3 * q + i].append(parts[i])
            for q in range(2):
                total = sums[3 * q]
                if ahead > 0:
                    total = [x + y for x, y in zip(total, moved_left(sums[3 * q + 1]))]
                if ahead < views:
                    total = [x + y for x, y in zip(total, moved_right(sums[3 * q + 2]))]
                for g in range(groups):
                    out_ref[q, b, pl.ds(g * GROUP + row, SUBS, stride=SUBS), :] = total[g]

        def body(i, carry):
            b = i // (SUBS // steps)
            first = lax.rem(i, SUBS // steps)
            for step in range(steps):
                cell(i * steps + step, b, first * steps + step)

            @pl.when(first == SUBS // steps - 1)
            def _():
                for copy in send(b):
                    copy.start()

            return carry

        lax.fori_loop(0, cells // steps, body, 0)

    for ahead in range(views + 1):

        @pl.when(count == ahead)
        def _():
            products(ahead)

    for b in range(cells // SUBS):
        for copy in send(b):
            copy.wait()


def on_device(density, attenuation, measured, angle_ids, sides):
    cells, columns = density.shape[1:]
    views = measured.shape[0]
    slabs, rows = lax.axis_size("depth"), lax.axis_size("rows")
    devices = slabs * rows
    assert views == 4 and slabs % views == 0 and cells % SUBS == 0 and columns % (SUBS * LANES) == 0
    part = columns // devices
    compact = slabs == SUBS and part == 2 * LANES
    blocks, tiles = cells // SUBS, columns // LANES
    groups, length, fields = tiles // SUBS, tiles * SUBS, views + 2
    vmem = pl.BlockSpec(memory_space=pltpu.VMEM)
    leave = pl.BlockSpec(memory_space=pl.ANY)

    def grant(mib):
        return pltpu.CompilerParams(vmem_limit_bytes=mib << 20)

    def in_hbm(x):
        return pltpu.with_memory_space_constraint(x, pltpu.HBM)

    def tiled(x):
        return x.reshape(blocks, SUBS, tiles, LANES).transpose(0, 2, 1, 3).reshape(blocks, length, LANES)

    def untiled(x):
        return x.reshape(blocks, tiles, SUBS, LANES).transpose(0, 2, 1, 3).reshape(1, cells, columns)

    ids_in = [in_hbm(angle_ids), in_hbm(sides)]
    ids = [pltpu.SMEM((views,), jnp.int32)] * 2
    field = pltpu.VMEM((2, views, cells, groups) + TILE, F32)
    shifted = pltpu.VMEM((3, cells, groups, SUBS, LANES), F32)
    up, tilts, light = pl.pallas_call(
        functools.partial(slab_kernel, views, slabs),
        out_shape=(pltpu.VMEM((tiles * fields, LANES), F32), pltpu.VMEM((3,) + TILE, F32), field),
        in_specs=[leave] * 5,
        out_specs=(vmem,) * 3,
        scratch_shapes=ids
        + [
            pltpu.VMEM((2, blocks, length, LANES), F32),
            shifted,
            shifted,
            pltpu.VMEM((groups,) + TILE, F32),
            pltpu.VMEM((tiles, LANES), F32),
            pltpu.SemaphoreType.DMA((3,)),
            pltpu.SemaphoreType.DMA((2, blocks)),
        ],
        compiler_params=grant(24),
        name="slab",
    )(
        *ids_in,
        in_hbm(tiled(density[0])),
        in_hbm(tiled(attenuation[0])),
        in_hbm(measured.reshape(views, tiles, LANES)),
    )

    def exchange(x):
        return lax.all_to_all(x, ("depth", "rows"), 0, 0, tiled=True)

    if compact:
        rows_of = (devices * 2 * fields // 4, 4, LANES)
        up = exchange(up.reshape(rows_of)).reshape(tiles * fields, LANES)
    else:
        flat = up.reshape(tiles, fields, LANES).transpose(1, 0, 2).reshape(fields, columns)
        total = flat[views : views + 1]
        order = jnp.argsort(sides, stable=True)
        place = lax.rem(lax.axis_index("depth") // (slabs // views), views)
        counts = lax.dynamic_index_in_dim(measured[:, 0], order[place], 0)
        before = jnp.pad(total[:, :-1], ((0, 0), (1, 0)))
        after = jnp.pad(total[:, 1:], ((0, 0), (0, 1)))
        flat = jnp.concatenate([flat[:views], before, total, after, counts], axis=0)
        up = exchange(flat.reshape(SUBS, devices, part).transpose(1, 0, 2))
    kernel = functools.partial(column_kernel, views, rows) if compact else functools.partial(wide_column_kernel, views, slabs, rows)
    down = pl.pallas_call(
        kernel,
        out_shape=pltpu.VMEM(up.shape, F32) if compact else jax.ShapeDtypeStruct(up.shape, F32),
        in_specs=[vmem] * 2,
        out_specs=vmem,
        compiler_params=grant(4 if compact else 16),
        name="column",
    )(tilts, up)
    if compact:
        down = exchange(down.reshape(rows_of)).reshape(tiles * fields, LANES)
    else:
        flat = exchange(down).transpose(1, 0, 2).reshape(SUBS, columns)
        base = flat[views] + jnp.pad(flat[views + 1, 1:], (0, 1)) + jnp.pad(flat[views + 2, :-1], (1, 0))
        flat = jnp.concatenate([flat[:views], base[None], jnp.zeros((1, columns), F32)], axis=0)
        down = flat.reshape(fields, tiles, LANES).transpose(1, 0, 2).reshape(tiles * fields, LANES)
    grads = pl.pallas_call(
        functools.partial(gradient_kernel, views),
        out_shape=(pltpu.HBM((blocks, length, LANES), F32),) * 2,
        in_specs=[vmem] * 3,
        out_specs=(leave,) * 2,
        scratch_shapes=[
            pltpu.VMEM((3, views, groups) + TILE, F32),
            pltpu.VMEM((2, blocks, length, LANES), F32),
            pltpu.SemaphoreType.DMA((2, blocks)),
        ],
        compiler_params=grant(8),
        name="gradient",
    )(tilts, down, light)
    return untiled(grads[0]), untiled(grads[1])


def solution(mesh):
    placed = (P("rows", "depth", None), P("rows", "depth", None), P(None, "rows", None), P(), P())
    return jax.shard_map(
        on_device,
        mesh=mesh,
        in_specs=placed,
        out_specs=(P("rows", "depth", None), P("rows", "depth", None)),
        check_vma=False,
    )
```

```python
import functools
import math

import jax
import jax.numpy as jnp
from jax import lax
from jax.experimental import pallas as pl
from jax.experimental.pallas import tpu as pltpu
from jax.sharding import PartitionSpec as P

ANGLES = 360
LANES, SUBS = 128, 8
GROUP = SUBS * SUBS
TILE = (SUBS, LANES)
F32 = jnp.float32


def tilt_parts(angle):
    tilt = 0.8 * jnp.sin(jnp.pi * (angle.astype(F32) + 0.5) / ANGLES - jnp.pi / 2)
    return 1.0 - jnp.abs(tilt), jnp.maximum(tilt, 0.0), jnp.maximum(-tilt, 0.0)


def leans_right(angle):
    return 2 * angle >= ANGLES


def near_first(sides, views):
    order = [0] * views
    seen = [jnp.int32(0), jnp.int32(views // 2)]
    for v in range(views):
        far = (sides[v] == 1).astype(jnp.int32)
        place = jnp.where(far == 1, seen[1], seen[0])
        seen = [seen[0] + 1 - far, seen[1] + far]
        order = [jnp.where(place == p, v, order[p]) for p in range(views)]
    return order


def lanes():
    return lax.broadcasted_iota(jnp.int32, TILE, 1)


def subs():
    return lax.broadcasted_iota(jnp.int32, TILE, 0)


def spread(row):
    return jnp.broadcast_to(row, TILE)


def moved_right(blocks, around=False):
    first_lane, first_sub = lanes() == 0, subs() == 0
    rolled = [pltpu.roll(x, 1, 1) for x in blocks]
    down = [pltpu.roll(x, 1, 0) for x in rolled]
    past = [down[-1] if around else jnp.zeros(TILE, F32)] + down[:-1]
    return [jnp.where(first_lane, jnp.where(first_sub, x, y), z) for x, y, z in zip(past, down, rolled)]


def moved_left(blocks, around=False):
    last_lane, last_sub = lanes() == LANES - 1, subs() == SUBS - 1
    rolled = [pltpu.roll(x, LANES - 1, 1) for x in blocks]
    up = [pltpu.roll(x, SUBS - 1, 0) for x in rolled]
    later = up[1:] + [up[0] if around else jnp.zeros(TILE, F32)]
    return [jnp.where(last_lane, jnp.where(last_sub, x, y), z) for x, y, z in zip(later, up, rolled)]


def slab_kernel(
    views, slabs, angle_hbm, side_hbm, d_hbm, a_hbm, m_hbm, up_ref, tilt_ref, field_ref,
    angle_ref, side_ref, raw_ref, ax_ref, dx_ref, sum_ref, front_ref, m_ref, sem, sem_raw,
):
    blocks, length = raw_ref.shape[1:3]
    cells, groups, fields = blocks * SUBS, length // GROUP, views + 2
    slab = lax.axis_index("depth")
    share = max(slabs // views, 1)

    def fetch(b):
        return [pltpu.make_async_copy(hbm.at[b], raw_ref.at[f, b], sem_raw.at[f, b]) for f, hbm in enumerate((a_hbm, d_hbm))]

    small = [pltpu.make_async_copy(angle_hbm, angle_ref, sem.at[0]), pltpu.make_async_copy(side_hbm, side_ref, sem.at[1])]
    for copy in small + [copy for b in range(blocks) for copy in fetch(b)]:
        copy.start()
    scale = -math.log2(math.e)
    corner = jnp.logical_and(lanes() == 0, subs() == 0)
    sum_ref[...] = jnp.zeros(sum_ref.shape, F32)

    steps = 8

    def shifts(i, carry):
        b = i // (SUBS // steps)
        first = lax.rem(i, SUBS // steps)

        @pl.when(first == 0)
        def _():
            for copy in fetch(b):
                copy.wait()

        sums = [sum_ref[g] for g in range(groups)]
        for step in range(steps):
            z, row = i * steps + step, first * steps + step
            for f, ref in enumerate((ax_ref, dx_ref)):
                values = [raw_ref[f, b, pl.ds(g * GROUP + row, SUBS, stride=SUBS), :] for g in range(groups)]
                if f == 0:
                    values = [scale * x for x in values]
                    sums = [x + y for x, y in zip(sums, values)]
                around = moved_right(values, around=True)
                for g, (here, left) in enumerate(zip(values, around)):
                    ref[0, z, g] = here
                    ref[1, z, g] = (jnp.where(corner, 0.0, left) if g == 0 else left) - here
                here = jnp.where(corner, 0.0, values[0])
                ref[0, z, groups] = here
                ref[1, z, groups] = around[0] - here
        for g in range(groups):
            sum_ref[g] = sums[g]
        return carry

    lax.fori_loop(0, cells // steps, shifts, 0)
    for copy in small:
        copy.wait()
    order = near_first(side_ref, views)
    seen = jnp.int32(0)
    for p in range(views):
        seen = jnp.where(lax.rem(slab // share, views) == p, order[p], seen)
    fetch_m = pltpu.make_async_copy(m_hbm.at[seen], m_ref, sem.at[2])
    fetch_m.start()
    angle_block = jnp.zeros(TILE, jnp.int32)
    for p in range(views):
        angle_block = jnp.where(subs() == p, angle_ref[order[p]], angle_block)
    parts = tilt_parts(angle_block)
    for i, part in enumerate(parts):
        tilt_ref[i] = part
    before_weight = jnp.where(parts[1] > 0.0, parts[1], parts[0])
    weights = [spread(before_weight[p : p + 1]) for p in range(views)]
    right = [leans_right(angle_ref[order[p]]) for p in range(views)]

    def put(g, field, value):
        up_ref[pl.ds(g * SUBS * fields + field, SUBS, stride=fields), :] = value

    abreast = 2

    def rays(i, carry):
        several = [i * abreast + j for j in range(abreast)]
        places = [[jnp.where(jnp.logical_or(right[p], g > 0), g, groups) for p in range(views)] for g in several]
        depth = {(j, p): jnp.zeros(TILE, F32) for j in range(abreast) for p in range(views)}
        front = dict(depth)
        for i in range(cells):
            for j, g in enumerate(several):
                for p in range(views):
                    z = i if p < views // 2 else cells - 1 - i
                    light = jnp.exp2(depth[j, p])
                    at = places[j][p]
                    depth[j, p] = depth[j, p] + (ax_ref[0, z, at] + weights[p] * ax_ref[1, z, at])
                    front[j, p] = front[j, p] + (dx_ref[0, z, at] + weights[p] * dx_ref[1, z, at]) * light
                    field_ref[0, p, z, g] = light
                    field_ref[1, p, z, g] = front[j, p]
        for j, g in enumerate(several):
            for p in range(views):
                front_ref[p, g] = front[j, p]
        return carry

    lax.fori_loop(0, groups // abreast, rays, 0)
    for p in range(views):
        own = [front_ref[p, g] for g in range(groups)]
        for g, (here, after) in enumerate(zip(own, moved_left(own, around=True))):
            put(g, p, jnp.where(right[p], here, after))
    fetch_m.wait()
    totals = [sum_ref[g] for g in range(groups)]
    odd = lax.rem(subs(), 2) == 1
    second = lax.rem(slab, share) == 1
    for g, (before, after) in enumerate(zip(moved_right(totals), moved_left(totals))):
        counts = m_ref[pl.ds(g * SUBS, SUBS), :]
        counts = jnp.where(second, pltpu.roll(counts, SUBS - 1, 0), counts)
        edges = jnp.where(lanes() == 0, pltpu.roll(before, 1, 0), after)
        put(g, views, totals[g])
        put(g, views + 1, jnp.where(odd, edges, counts))


def blur(values):
    out = []
    for r in range(len(values)):
        total = 0.5 * values[r]
        if r > 0:
            total = total + 0.25 * values[r - 1]
        if r + 1 < len(values):
            total = total + 0.25 * values[r + 1]
        out.append(total)
    return out


def column_kernel(views, rows, tilt_ref, up_ref, down_ref):
    fields = views + 2
    record = 2 * fields
    first_lane, last_lane, sub = lanes() == 0, lanes() == LANES - 1, subs()
    weights = [[spread(tilt_ref[i, p : p + 1]) for i in range(3)] for p in range(views)]

    def get(r, half, field):
        return up_ref[pl.ds(r * record + half * fields + field, SUBS, stride=rows * record), :]

    def put(r, half, field, value):
        down_ref[pl.ds(r * record + half * fields + field, SUBS, stride=rows * record), :] = value

    def scan(value, far):
        step = 1
        while step < SUBS:
            if far:
                value = value + jnp.where(sub >= step, pltpu.roll(value, step, 0), 0.0)
            else:
                value = value + jnp.where(sub < SUBS - step, pltpu.roll(value, SUBS - step, 0), 0.0)
            step *= 2
        return value

    passes, behinds = {}, {}
    signals = {(p, half): [] for p in range(views) for half in range(2)}
    for r in range(rows):
        total = [get(r, half, views) for half in range(2)]
        edges = get(r, 1, views + 1)
        up = [pltpu.roll(x, 1, 1) for x in total]
        down = [pltpu.roll(x, LANES - 1, 1) for x in total]
        before = [jnp.where(first_lane, edges, up[0]), jnp.where(first_lane, up[0], up[1])]
        after = [jnp.where(last_lane, down[1], down[0]), jnp.where(last_lane, edges, down[1])]
        for half in range(2):
            for p in range(views):
                far = p >= views // 2
                centre, left, right = weights[p]
                absorb = centre * total[half] + left * before[half] + right * after[half]
                entering = scan(absorb, not far) - absorb
                light = jnp.exp2(entering)
                behind = scan(light * get(r, half, p), far)
                passes[r, half, p] = light
                behinds[r, half, p] = behind
                edge = SUBS - 1 if far else 0
                signals[p, half].append(spread(behind[edge : edge + 1]))
    backs = {}
    for p in range(views):
        for half in range(2):
            residuals = []
            for r, value in enumerate(blur(signals[p, half])):
                at = ((p * (SUBS // views) + half) * rows + r) * record + views + 1
                residuals.append(value - spread(up_ref[pl.ds(at, 1), :]))
            backs[p, half] = blur(residuals)
    for r in range(rows):
        sums = []
        for half in range(2):
            parts = [jnp.zeros(TILE, F32)] * 3
            for p in range(views):
                back = backs[p, half][r]
                put(r, half, p, back * passes[r, half, p])
                scaled = back * behinds[r, half, p]
                parts = [part - weight * scaled for part, weight in zip(parts, weights[p])]
            sums.append(parts)
        next_up = [pltpu.roll(sums[half][1], LANES - 1, 1) for half in range(2)]
        previous = [pltpu.roll(sums[half][2], 1, 1) for half in range(2)]
        zero = jnp.zeros(TILE, F32)
        put(r, 0, views, sums[0][0] + jnp.where(last_lane, next_up[1], next_up[0]) + jnp.where(first_lane, zero, previous[0]))
        put(r, 1, views, sums[1][0] + jnp.where(last_lane, zero, next_up[1]) + jnp.where(first_lane, previous[0], previous[1]))
        put(r, 0, views + 1, jnp.where(last_lane, next_up[0], zero))
        put(r, 1, views + 1, jnp.where(first_lane, previous[1], zero))


def wide_column_kernel(views, slabs, rows, tilt_ref, up_ref, down_ref):
    wide = up_ref.shape[2]
    shape = (views, wide)
    centre, left, right = [tilt_ref[i, :views, :1] for i in range(3)]
    far = lax.broadcasted_iota(jnp.int32, shape, 0) >= views // 2
    passes, behinds, signals = {}, {}, []
    for r in range(rows):
        absorbs, runs = [], []
        run = jnp.zeros(shape, F32)
        for k in range(slabs):
            block = up_ref[k * rows + r]
            absorb = left * block[views : views + 1] + centre * block[views + 1 : views + 2] + right * block[views + 2 : views + 3]
            runs.append(run)
            absorbs.append(absorb)
            run = run + absorb
        ends, starts = [], []
        signal = jnp.zeros(shape, F32)
        for k in range(slabs):
            entering = jnp.where(far, run - runs[k] - absorbs[k], runs[k])
            passes[k, r] = jnp.exp2(entering)
            starts.append(signal)
            signal = signal + passes[k, r] * up_ref[k * rows + r, :views]
            ends.append(signal)
        for k in range(slabs):
            behinds[k, r] = jnp.where(far, -ends[k], starts[k] - signal)
        signals.append(signal)
    residuals = []
    for r, value in enumerate(blur(signals)):
        seen = [up_ref[(v * max(slabs // views, 1)) * rows + r, views + 3 : views + 4] for v in range(views)]
        residuals.append(value - jnp.concatenate(seen, axis=0))
    for r, back in enumerate(blur(residuals)):
        for k in range(slabs):
            scaled = back * behinds[k, r]
            parts = [back * passes[k, r]]
            for weight in (centre, left, right):
                parts.append(jnp.sum(weight * scaled, axis=0, keepdims=True))
            parts.append(jnp.zeros((1, wide), F32))
            down_ref[k * rows + r] = jnp.concatenate(parts, axis=0)


def gradient_kernel(views, tilt_ref, down_ref, field_ref, gd_hbm, ga_hbm, scale_ref, out_ref, sem_out):
    cells, groups = field_ref.shape[2:4]
    fields = views + 2

    def send(b):
        return [pltpu.make_async_copy(out_ref.at[q, b], hbm.at[b], sem_out.at[q, b]) for q, hbm in enumerate((gd_hbm, ga_hbm))]

    def get(g, field):
        return down_ref[pl.ds(g * SUBS * fields + field, SUBS, stride=fields), :]

    corner = jnp.logical_and(lanes() == 0, subs() == 0)
    for p in range(views):
        centre, left, right = [spread(tilt_ref[i, p : p + 1]) for i in range(3)]
        leans = left > 0.0
        own = [get(g, p) for g in range(groups)]
        for g, (here, before) in enumerate(zip(own, moved_right(own, around=True))):
            back = jnp.where(leans, here, before)
            inner, outer = centre * back, (left + right) * back
            if g == 0:
                outer = jnp.where(corner, 0.0, outer)
            scale_ref[0, p, g] = jnp.where(leans, inner, outer)
            scale_ref[1, p, g] = jnp.where(leans, outer, inner)
    odd = lax.rem(subs(), 2) == 1
    extras = [get(g, views + 1) for g in range(groups)]
    zero = jnp.zeros(TILE, F32)
    for g in range(groups):
        later = pltpu.roll(extras[g], SUBS - 1, 0)
        ahead = pltpu.roll(extras[g + 1], SUBS - 1, 0) if g + 1 < groups else zero
        later = jnp.where(subs() == SUBS - 1, ahead, later)
        earlier = pltpu.roll(extras[g], 1, 0)
        past = pltpu.roll(extras[g - 1], 1, 0) if g > 0 else zero
        earlier = jnp.where(subs() == 0, past, earlier)
        scale_ref[2, 0, g] = get(g, views) + jnp.where(odd, later, earlier)

    steps = 8

    def cell(z, b, row):
        for q in range(2):
            sums = [[], []]
            for g in range(groups):
                values = [field_ref[q, p, z, g] for p in range(views)]
                for i in range(2):
                    terms = [scale_ref[i, p, g] * value for p, value in enumerate(values)]
                    if q == 1 and i == 0:
                        terms[0] = terms[0] + scale_ref[2, 0, g]
                    sums[i].append((terms[0] + terms[1]) + (terms[2] + terms[3]))
            for g, (here, after) in enumerate(zip(sums[0], moved_left(sums[1], around=True))):
                out_ref[q, b, pl.ds(g * GROUP + row, SUBS, stride=SUBS), :] = here + after

    def body(i, carry):
        b = i // (SUBS // steps)
        first = lax.rem(i, SUBS // steps)
        for step in range(steps):
            cell(i * steps + step, b, first * steps + step)

        @pl.when(first == SUBS // steps - 1)
        def _():
            for copy in send(b):
                copy.start()

        return carry

    lax.fori_loop(0, cells // steps, body, 0)
    for b in range(cells // SUBS):
        for copy in send(b):
            copy.wait()


def on_device(density, attenuation, measured, angle_ids, sides):
    cells, columns = density.shape[1:]
    views = measured.shape[0]
    slabs, rows = lax.axis_size("depth"), lax.axis_size("rows")
    devices = slabs * rows
    assert views == 4 and slabs % views == 0 and cells % SUBS == 0 and columns % (SUBS * LANES) == 0
    part = columns // devices
    compact = slabs == SUBS and part == 2 * LANES
    blocks, tiles = cells // SUBS, columns // LANES
    groups, length, fields = tiles // SUBS, tiles * SUBS, views + 2
    vmem = pl.BlockSpec(memory_space=pltpu.VMEM)
    leave = pl.BlockSpec(memory_space=pl.ANY)

    def grant(mib):
        return pltpu.CompilerParams(vmem_limit_bytes=mib << 20)

    def in_hbm(x):
        return pltpu.with_memory_space_constraint(x, pltpu.HBM)

    def tiled(x):
        return x.reshape(blocks, SUBS, tiles, LANES).transpose(0, 2, 1, 3).reshape(blocks, length, LANES)

    def untiled(x):
        return x.reshape(blocks, tiles, SUBS, LANES).transpose(0, 2, 1, 3).reshape(1, cells, columns)

    ids_in = [in_hbm(angle_ids), in_hbm(sides)]
    ids = [pltpu.SMEM((views,), jnp.int32)] * 2
    field = pltpu.VMEM((2, views, cells, groups) + TILE, F32)
    shifted = pltpu.VMEM((2, cells, groups + 1) + TILE, F32)
    up, tilts, light = pl.pallas_call(
        functools.partial(slab_kernel, views, slabs),
        out_shape=(pltpu.VMEM((tiles * fields, LANES), F32), pltpu.VMEM((3,) + TILE, F32), field),
        in_specs=[leave] * 5,
        out_specs=(vmem,) * 3,
        scratch_shapes=ids
        + [
            pltpu.VMEM((2, blocks, length, LANES), F32),
            shifted,
            shifted,
            pltpu.VMEM((groups,) + TILE, F32),
            pltpu.VMEM((views, groups) + TILE, F32),
            pltpu.VMEM((tiles, LANES), F32),
            pltpu.SemaphoreType.DMA((3,)),
            pltpu.SemaphoreType.DMA((2, blocks)),
        ],
        compiler_params=grant(24),
        name="slab",
    )(
        *ids_in,
        in_hbm(tiled(density[0])),
        in_hbm(tiled(attenuation[0])),
        in_hbm(measured.reshape(views, tiles, LANES)),
    )

    def exchange(x):
        return lax.all_to_all(x, ("depth", "rows"), 0, 0, tiled=True)

    if compact:
        rows_of = (devices * 2 * fields // 4, 4, LANES)
        up = exchange(up.reshape(rows_of)).reshape(tiles * fields, LANES)
    else:
        flat = up.reshape(tiles, fields, LANES).transpose(1, 0, 2).reshape(fields, columns)
        total = flat[views : views + 1]
        order = jnp.argsort(sides, stable=True)
        place = lax.rem(lax.axis_index("depth") // (slabs // views), views)
        counts = lax.dynamic_index_in_dim(measured[:, 0], order[place], 0)
        before = jnp.pad(total[:, :-1], ((0, 0), (1, 0)))
        after = jnp.pad(total[:, 1:], ((0, 0), (0, 1)))
        flat = jnp.concatenate([flat[:views], before, total, after, counts], axis=0)
        up = exchange(flat.reshape(SUBS, devices, part).transpose(1, 0, 2))
    kernel = functools.partial(column_kernel, views, rows) if compact else functools.partial(wide_column_kernel, views, slabs, rows)
    down = pl.pallas_call(
        kernel,
        out_shape=pltpu.VMEM(up.shape, F32) if compact else jax.ShapeDtypeStruct(up.shape, F32),
        in_specs=[vmem] * 2,
        out_specs=vmem,
        compiler_params=grant(4 if compact else 16),
        name="column",
    )(tilts, up)
    if compact:
        down = exchange(down.reshape(rows_of)).reshape(tiles * fields, LANES)
    else:
        flat = exchange(down).transpose(1, 0, 2).reshape(SUBS, columns)
        base = flat[views] + jnp.pad(flat[views + 1, 1:], (0, 1)) + jnp.pad(flat[views + 2, :-1], (1, 0))
        flat = jnp.concatenate([flat[:views], base[None], jnp.zeros((1, columns), F32)], axis=0)
        down = flat.reshape(fields, tiles, LANES).transpose(1, 0, 2).reshape(tiles * fields, LANES)
    grads = pl.pallas_call(
        functools.partial(gradient_kernel, views),
        out_shape=(pltpu.HBM((blocks, length, LANES), F32),) * 2,
        in_specs=[vmem] * 3,
        out_specs=(leave,) * 2,
        scratch_shapes=[
            pltpu.VMEM((3, views, groups) + TILE, F32),
            pltpu.VMEM((2, blocks, length, LANES), F32),
            pltpu.SemaphoreType.DMA((2, blocks)),
        ],
        compiler_params=grant(8),
        name="gradient",
    )(tilts, down, light)
    return untiled(grads[0]), untiled(grads[1])


def solution(mesh):
    placed = (P("rows", "depth", None), P("rows", "depth", None), P(None, "rows", None), P(), P())
    return jax.shard_map(
        on_device,
        mesh=mesh,
        in_specs=placed,
        out_specs=(P("rows", "depth", None), P("rows", "depth", None)),
        check_vma=False,
    )
```

```python
import functools
import math

import jax
import jax.numpy as jnp
from jax import lax
from jax.experimental import pallas as pl
from jax.experimental.pallas import tpu as pltpu
from jax.sharding import PartitionSpec as P

ANGLES = 360
LANES, SUBS = 128, 8
GROUP = SUBS * SUBS
ABREAST = 2
TILE = (SUBS, LANES)
F32 = jnp.float32


def tilt_parts(angle):
    tilt = 0.8 * jnp.sin(jnp.pi * (angle.astype(F32) + 0.5) / ANGLES - jnp.pi / 2)
    return 1.0 - jnp.abs(tilt), jnp.maximum(tilt, 0.0), jnp.maximum(-tilt, 0.0)


def leans_right(angle):
    return 2 * angle >= ANGLES


def near_first(sides, views):
    order = [0] * views
    seen = [jnp.int32(0), jnp.int32(views // 2)]
    for v in range(views):
        far = (sides[v] == 1).astype(jnp.int32)
        place = jnp.where(far == 1, seen[1], seen[0])
        seen = [seen[0] + 1 - far, seen[1] + far]
        order = [jnp.where(place == p, v, order[p]) for p in range(views)]
    return order


def lanes():
    return lax.broadcasted_iota(jnp.int32, TILE, 1)


def subs():
    return lax.broadcasted_iota(jnp.int32, TILE, 0)


def spread(row):
    return jnp.broadcast_to(row, TILE)


def moved_right(blocks, around=False):
    first_lane, first_sub = lanes() == 0, subs() == 0
    rolled = [pltpu.roll(x, 1, 1) for x in blocks]
    down = [pltpu.roll(x, 1, 0) for x in rolled]
    past = [down[-1] if around else jnp.zeros(TILE, F32)] + down[:-1]
    return [jnp.where(first_lane, jnp.where(first_sub, x, y), z) for x, y, z in zip(past, down, rolled)]


def moved_left(blocks, around=False):
    last_lane, last_sub = lanes() == LANES - 1, subs() == SUBS - 1
    rolled = [pltpu.roll(x, LANES - 1, 1) for x in blocks]
    up = [pltpu.roll(x, SUBS - 1, 0) for x in rolled]
    later = up[1:] + [up[0] if around else jnp.zeros(TILE, F32)]
    return [jnp.where(last_lane, jnp.where(last_sub, x, y), z) for x, y, z in zip(later, up, rolled)]


def slab_kernel(
    views, slabs, angle_hbm, side_hbm, d_hbm, a_hbm, m_hbm, up_ref, tilt_ref, field_ref,
    angle_ref, side_ref, raw_ref, tail_ref, even_ref, odd_ref, last_ref, front_ref, m_ref, sem, sem_raw,
):
    blocks, length = raw_ref.shape[1:3]
    cells, groups, fields = blocks * SUBS, length // GROUP, views + 2
    slab = lax.axis_index("depth")
    share = max(slabs // views, 1)
    abreast = even_ref.shape[3] - 1
    turns = groups // abreast
    scale = -math.log2(math.e)
    factors = (scale, 1.0)
    first_lane, first_sub = lanes() == 0, subs() == 0
    corner = jnp.logical_and(first_lane, first_sub)

    def fetch(turn):
        part = pl.ds(turn * abreast * GROUP, abreast * GROUP)
        return [
            pltpu.make_async_copy(hbm.at[:, part], raw_ref.at[f, :, part], sem_raw.at[f, turn])
            for f, hbm in enumerate((a_hbm, d_hbm))
        ]

    ends = [
        pltpu.make_async_copy(hbm.at[:, pl.ds(length - SUBS, SUBS)], tail_ref.at[f], sem_raw.at[f, turns])
        for f, hbm in enumerate((a_hbm, d_hbm))
    ]
    small = [pltpu.make_async_copy(angle_hbm, angle_ref, sem.at[0]), pltpu.make_async_copy(side_hbm, side_ref, sem.at[1])]
    for copy in ends + fetch(0) + small + [copy for turn in range(1, turns) for copy in fetch(turn)]:
        copy.start()

    def shift(turn, ref, f, z, ending=None):
        b, row = z // SUBS, z % SUBS
        past = jnp.zeros(TILE, F32) if turn == 0 else last_ref[f, z]
        for j in range(abreast):
            here = raw_ref[f, b, pl.ds((turn * abreast + j) * GROUP + row, SUBS, stride=SUBS), :]
            if f == 0:
                here = scale * here
            rolled = pltpu.roll(here, 1, 1)
            down = pltpu.roll(rolled, 1, 0)
            ref[f, 0, z, j] = here
            ref[f, 1, z, j] = jnp.where(first_lane, jnp.where(first_sub, past, down), rolled) - here
            if turn == 0 and j == 0:
                inner = jnp.where(corner, 0.0, here)
                ref[f, 0, z, abreast] = inner
                ref[f, 1, z, abreast] = jnp.where(first_lane, jnp.where(first_sub, ending, down), rolled) - inner
            if f == 0:
                sums[turn * abreast + j] = here if sums[turn * abreast + j] is None else sums[turn * abreast + j] + here
            past = down
        if turn + 1 < turns:
            last_ref[f, z] = past

    sums = [None] * groups
    for copy in ends + fetch(0):
        copy.wait()
    for f in range(2):
        for b in range(blocks):
            turned = factors[f] * pltpu.roll(tail_ref[f, b], 1, 1)
            for row in range(SUBS):
                shift(0, even_ref, f, b * SUBS + row, spread(turned[row : row + 1]))

    for copy in small:
        copy.wait()
    order = near_first(side_ref, views)
    seen = jnp.int32(0)
    for p in range(views):
        seen = jnp.where(lax.rem(slab // share, views) == p, order[p], seen)
    fetch_m = pltpu.make_async_copy(m_hbm.at[seen], m_ref, sem.at[2])
    fetch_m.start()
    angle_block = jnp.zeros(TILE, jnp.int32)
    for p in range(views):
        angle_block = jnp.where(subs() == p, angle_ref[order[p]], angle_block)
    parts = tilt_parts(angle_block)
    for i, part in enumerate(parts):
        tilt_ref[i] = part
    before_weight = jnp.where(parts[1] > 0.0, parts[1], parts[0])
    weights = [spread(before_weight[p : p + 1]) for p in range(views)]
    right = [leans_right(angle_ref[order[p]]) for p in range(views)]

    def put(g, field, value):
        up_ref[pl.ds(g * SUBS * fields + field, SUBS, stride=fields), :] = value

    for turn in range(turns):
        ref, other = (even_ref, odd_ref) if turn % 2 == 0 else (odd_ref, even_ref)
        if turn + 1 < turns:
            for copy in fetch(turn + 1):
                copy.wait()
        depth = {(j, p): jnp.zeros(TILE, F32) for j in range(abreast) for p in range(views)}
        front = dict(depth)
        for i in range(cells):
            for j in range(abreast):
                g = turn * abreast + j
                for p in range(views):
                    z = i if p < views // 2 else cells - 1 - i
                    at = jnp.where(right[p], 0, abreast) if g == 0 else j
                    light = jnp.exp2(depth[j, p])
                    depth[j, p] = depth[j, p] + (ref[0, 0, z, at] + weights[p] * ref[0, 1, z, at])
                    front[j, p] = front[j, p] + (ref[1, 0, z, at] + weights[p] * ref[1, 1, z, at]) * light
                    field_ref[0, p, z, g] = light
                    field_ref[1, p, z, g] = front[j, p]
            if turn + 1 < turns:
                for f in range(2):
                    shift(turn + 1, other, f, i)
        for j in range(abreast):
            for p in range(views):
                front_ref[p, turn * abreast + j] = front[j, p]

    for p in range(views):
        own = [front_ref[p, g] for g in range(groups)]
        for g, (here, after) in enumerate(zip(own, moved_left(own, around=True))):
            put(g, p, jnp.where(right[p], here, after))
    fetch_m.wait()
    odd = lax.rem(subs(), 2) == 1
    second = lax.rem(slab, share) == 1
    for g, (before, after) in enumerate(zip(moved_right(sums), moved_left(sums))):
        counts = m_ref[pl.ds(g * SUBS, SUBS), :]
        counts = jnp.where(second, pltpu.roll(counts, SUBS - 1, 0), counts)
        edges = jnp.where(first_lane, pltpu.roll(before, 1, 0), after)
        put(g, views, sums[g])
        put(g, views + 1, jnp.where(odd, edges, counts))


def blur(values):
    out = []
    for r in range(len(values)):
        total = 0.5 * values[r]
        if r > 0:
            total = total + 0.25 * values[r - 1]
        if r + 1 < len(values):
            total = total + 0.25 * values[r + 1]
        out.append(total)
    return out


def column_kernel(views, rows, tilt_ref, up_ref, down_ref):
    fields = views + 2
    record = 2 * fields
    first_lane, last_lane, sub = lanes() == 0, lanes() == LANES - 1, subs()
    weights = [[spread(tilt_ref[i, p : p + 1]) for i in range(3)] for p in range(views)]

    def get(r, half, field):
        return up_ref[pl.ds(r * record + half * fields + field, SUBS, stride=rows * record), :]

    def put(r, half, field, value):
        down_ref[pl.ds(r * record + half * fields + field, SUBS, stride=rows * record), :] = value

    def scan(value, far):
        step = 1
        while step < SUBS:
            if far:
                value = value + jnp.where(sub >= step, pltpu.roll(value, step, 0), 0.0)
            else:
                value = value + jnp.where(sub < SUBS - step, pltpu.roll(value, SUBS - step, 0), 0.0)
            step *= 2
        return value

    passes, behinds = {}, {}
    signals = {(p, half): [] for p in range(views) for half in range(2)}
    for r in range(rows):
        total = [get(r, half, views) for half in range(2)]
        edges = get(r, 1, views + 1)
        up = [pltpu.roll(x, 1, 1) for x in total]
        down = [pltpu.roll(x, LANES - 1, 1) for x in total]
        before = [jnp.where(first_lane, edges, up[0]), jnp.where(first_lane, up[0], up[1])]
        after = [jnp.where(last_lane, down[1], down[0]), jnp.where(last_lane, edges, down[1])]
        for half in range(2):
            for p in range(views):
                far = p >= views // 2
                centre, left, right = weights[p]
                absorb = centre * total[half] + left * before[half] + right * after[half]
                entering = scan(absorb, not far) - absorb
                light = jnp.exp2(entering)
                behind = scan(light * get(r, half, p), far)
                passes[r, half, p] = light
                behinds[r, half, p] = behind
                edge = SUBS - 1 if far else 0
                signals[p, half].append(spread(behind[edge : edge + 1]))
    backs = {}
    for p in range(views):
        for half in range(2):
            residuals = []
            for r, value in enumerate(blur(signals[p, half])):
                at = ((p * (SUBS // views) + half) * rows + r) * record + views + 1
                residuals.append(value - spread(up_ref[pl.ds(at, 1), :]))
            backs[p, half] = blur(residuals)
    for r in range(rows):
        sums = []
        for half in range(2):
            parts = [jnp.zeros(TILE, F32)] * 3
            for p in range(views):
                back = backs[p, half][r]
                put(r, half, p, back * passes[r, half, p])
                scaled = back * behinds[r, half, p]
                parts = [part - weight * scaled for part, weight in zip(parts, weights[p])]
            sums.append(parts)
        next_up = [pltpu.roll(sums[half][1], LANES - 1, 1) for half in range(2)]
        previous = [pltpu.roll(sums[half][2], 1, 1) for half in range(2)]
        zero = jnp.zeros(TILE, F32)
        put(r, 0, views, sums[0][0] + jnp.where(last_lane, next_up[1], next_up[0]) + jnp.where(first_lane, zero, previous[0]))
        put(r, 1, views, sums[1][0] + jnp.where(last_lane, zero, next_up[1]) + jnp.where(first_lane, previous[0], previous[1]))
        put(r, 0, views + 1, jnp.where(last_lane, next_up[0], zero))
        put(r, 1, views + 1, jnp.where(first_lane, previous[1], zero))


def wide_column_kernel(views, slabs, rows, tilt_ref, up_ref, down_ref):
    wide = up_ref.shape[2]
    shape = (views, wide)
    centre, left, right = [tilt_ref[i, :views, :1] for i in range(3)]
    far = lax.broadcasted_iota(jnp.int32, shape, 0) >= views // 2
    passes, behinds, signals = {}, {}, []
    for r in range(rows):
        absorbs, runs = [], []
        run = jnp.zeros(shape, F32)
        for k in range(slabs):
            block = up_ref[k * rows + r]
            absorb = left * block[views : views + 1] + centre * block[views + 1 : views + 2] + right * block[views + 2 : views + 3]
            runs.append(run)
            absorbs.append(absorb)
            run = run + absorb
        ends, starts = [], []
        signal = jnp.zeros(shape, F32)
        for k in range(slabs):
            entering = jnp.where(far, run - runs[k] - absorbs[k], runs[k])
            passes[k, r] = jnp.exp2(entering)
            starts.append(signal)
            signal = signal + passes[k, r] * up_ref[k * rows + r, :views]
            ends.append(signal)
        for k in range(slabs):
            behinds[k, r] = jnp.where(far, -ends[k], starts[k] - signal)
        signals.append(signal)
    residuals = []
    for r, value in enumerate(blur(signals)):
        seen = [up_ref[(v * max(slabs // views, 1)) * rows + r, views + 3 : views + 4] for v in range(views)]
        residuals.append(value - jnp.concatenate(seen, axis=0))
    for r, back in enumerate(blur(residuals)):
        for k in range(slabs):
            scaled = back * behinds[k, r]
            parts = [back * passes[k, r]]
            for weight in (centre, left, right):
                parts.append(jnp.sum(weight * scaled, axis=0, keepdims=True))
            parts.append(jnp.zeros((1, wide), F32))
            down_ref[k * rows + r] = jnp.concatenate(parts, axis=0)


def gradient_kernel(views, tilt_ref, down_ref, field_ref, gd_hbm, ga_hbm, scale_ref, out_ref, sem_out):
    cells, groups = field_ref.shape[2:4]
    fields = views + 2

    def send(b):
        return [pltpu.make_async_copy(out_ref.at[q, b], hbm.at[b], sem_out.at[q, b]) for q, hbm in enumerate((gd_hbm, ga_hbm))]

    def get(g, field):
        return down_ref[pl.ds(g * SUBS * fields + field, SUBS, stride=fields), :]

    corner = jnp.logical_and(lanes() == 0, subs() == 0)
    for p in range(views):
        centre, left, right = [spread(tilt_ref[i, p : p + 1]) for i in range(3)]
        leans = left > 0.0
        own = [get(g, p) for g in range(groups)]
        for g, (here, before) in enumerate(zip(own, moved_right(own, around=True))):
            back = jnp.where(leans, here, before)
            inner, outer = centre * back, (left + right) * back
            if g == 0:
                outer = jnp.where(corner, 0.0, outer)
            scale_ref[0, p, g] = jnp.where(leans, inner, outer)
            scale_ref[1, p, g] = jnp.where(leans, outer, inner)
    odd = lax.rem(subs(), 2) == 1
    extras = [get(g, views + 1) for g in range(groups)]
    zero = jnp.zeros(TILE, F32)
    for g in range(groups):
        later = pltpu.roll(extras[g], SUBS - 1, 0)
        ahead = pltpu.roll(extras[g + 1], SUBS - 1, 0) if g + 1 < groups else zero
        later = jnp.where(subs() == SUBS - 1, ahead, later)
        earlier = pltpu.roll(extras[g], 1, 0)
        past = pltpu.roll(extras[g - 1], 1, 0) if g > 0 else zero
        earlier = jnp.where(subs() == 0, past, earlier)
        scale_ref[2, 0, g] = get(g, views) + jnp.where(odd, later, earlier)

    steps = 8

    def cell(z, b, row):
        for q in range(2):
            sums = [[], []]
            for g in range(groups):
                values = [field_ref[q, p, z, g] for p in range(views)]
                for i in range(2):
                    terms = [scale_ref[i, p, g] * value for p, value in enumerate(values)]
                    if q == 1 and i == 0:
                        terms[0] = terms[0] + scale_ref[2, 0, g]
                    sums[i].append((terms[0] + terms[1]) + (terms[2] + terms[3]))
            for g, (here, after) in enumerate(zip(sums[0], moved_left(sums[1], around=True))):
                out_ref[q, b, pl.ds(g * GROUP + row, SUBS, stride=SUBS), :] = here + after

    def body(i, carry):
        b = i // (SUBS // steps)
        first = lax.rem(i, SUBS // steps)
        for step in range(steps):
            cell(i * steps + step, b, first * steps + step)

        @pl.when(first == SUBS // steps - 1)
        def _():
            for copy in send(b):
                copy.start()

        return carry

    lax.fori_loop(0, cells // steps, body, 0)
    for b in range(cells // SUBS):
        for copy in send(b):
            copy.wait()


def on_device(density, attenuation, measured, angle_ids, sides):
    cells, columns = density.shape[1:]
    views = measured.shape[0]
    slabs, rows = lax.axis_size("depth"), lax.axis_size("rows")
    devices = slabs * rows
    assert views == 4 and slabs % views == 0 and cells % SUBS == 0 and columns % (ABREAST * SUBS * LANES) == 0
    part = columns // devices
    compact = slabs == SUBS and part == 2 * LANES
    blocks, tiles = cells // SUBS, columns // LANES
    groups, length, fields = tiles // SUBS, tiles * SUBS, views + 2
    vmem = pl.BlockSpec(memory_space=pltpu.VMEM)
    leave = pl.BlockSpec(memory_space=pl.ANY)

    def grant(mib):
        return pltpu.CompilerParams(vmem_limit_bytes=mib << 20)

    def in_hbm(x):
        return pltpu.with_memory_space_constraint(x, pltpu.HBM)

    def tiled(x):
        return x.reshape(blocks, SUBS, tiles, LANES).transpose(0, 2, 1, 3).reshape(blocks, length, LANES)

    def untiled(x):
        return x.reshape(blocks, tiles, SUBS, LANES).transpose(0, 2, 1, 3).reshape(1, cells, columns)

    ids_in = [in_hbm(angle_ids), in_hbm(sides)]
    ids = [pltpu.SMEM((views,), jnp.int32)] * 2
    field = pltpu.VMEM((2, views, cells, groups) + TILE, F32)
    up, tilts, light = pl.pallas_call(
        functools.partial(slab_kernel, views, slabs),
        out_shape=(pltpu.VMEM((tiles * fields, LANES), F32), pltpu.VMEM((3,) + TILE, F32), field),
        in_specs=[leave] * 5,
        out_specs=(vmem,) * 3,
        scratch_shapes=ids
        + [
            pltpu.VMEM((2, blocks, length, LANES), F32),
            pltpu.VMEM((2, blocks) + TILE, F32),
            pltpu.VMEM((2, 2, cells, ABREAST + 1) + TILE, F32),
            pltpu.VMEM((2, 2, cells, ABREAST + 1) + TILE, F32),
            pltpu.VMEM((2, cells) + TILE, F32),
            pltpu.VMEM((views, groups) + TILE, F32),
            pltpu.VMEM((tiles, LANES), F32),
            pltpu.SemaphoreType.DMA((3,)),
            pltpu.SemaphoreType.DMA((2, groups // ABREAST + 1)),
        ],
        compiler_params=grant(24),
        name="slab",
    )(
        *ids_in,
        in_hbm(tiled(density[0])),
        in_hbm(tiled(attenuation[0])),
        in_hbm(measured.reshape(views, tiles, LANES)),
    )

    def exchange(x):
        return lax.all_to_all(x, ("depth", "rows"), 0, 0, tiled=True)

    if compact:
        rows_of = (devices * 2 * fields // 4, 4, LANES)
        up = exchange(up.reshape(rows_of)).reshape(tiles * fields, LANES)
    else:
        flat = up.reshape(tiles, fields, LANES).transpose(1, 0, 2).reshape(fields, columns)
        total = flat[views : views + 1]
        order = jnp.argsort(sides, stable=True)
        place = lax.rem(lax.axis_index("depth") // (slabs // views), views)
        counts = lax.dynamic_index_in_dim(measured[:, 0], order[place], 0)
        before = jnp.pad(total[:, :-1], ((0, 0), (1, 0)))
        after = jnp.pad(total[:, 1:], ((0, 0), (0, 1)))
        flat = jnp.concatenate([flat[:views], before, total, after, counts], axis=0)
        up = exchange(flat.reshape(SUBS, devices, part).transpose(1, 0, 2))
    kernel = functools.partial(column_kernel, views, rows) if compact else functools.partial(wide_column_kernel, views, slabs, rows)
    down = pl.pallas_call(
        kernel,
        out_shape=pltpu.VMEM(up.shape, F32) if compact else jax.ShapeDtypeStruct(up.shape, F32),
        in_specs=[vmem] * 2,
        out_specs=vmem,
        compiler_params=grant(4 if compact else 16),
        name="column",
    )(tilts, up)
    if compact:
        down = exchange(down.reshape(rows_of)).reshape(tiles * fields, LANES)
    else:
        flat = exchange(down).transpose(1, 0, 2).reshape(SUBS, columns)
        base = flat[views] + jnp.pad(flat[views + 1, 1:], (0, 1)) + jnp.pad(flat[views + 2, :-1], (1, 0))
        flat = jnp.concatenate([flat[:views], base[None], jnp.zeros((1, columns), F32)], axis=0)
        down = flat.reshape(fields, tiles, LANES).transpose(1, 0, 2).reshape(tiles * fields, LANES)
    grads = pl.pallas_call(
        functools.partial(gradient_kernel, views),
        out_shape=(pltpu.HBM((blocks, length, LANES), F32),) * 2,
        in_specs=[vmem] * 3,
        out_specs=(leave,) * 2,
        scratch_shapes=[
            pltpu.VMEM((3, views, groups) + TILE, F32),
            pltpu.VMEM((2, blocks, length, LANES), F32),
            pltpu.SemaphoreType.DMA((2, blocks)),
        ],
        compiler_params=grant(8),
        name="gradient",
    )(tilts, down, light)
    return untiled(grads[0]), untiled(grads[1])


def solution(mesh):
    placed = (P("rows", "depth", None), P("rows", "depth", None), P(None, "rows", None), P(), P())
    return jax.shard_map(
        on_device,
        mesh=mesh,
        in_specs=placed,
        out_specs=(P("rows", "depth", None), P("rows", "depth", None)),
        check_vma=False,
    )
```
